32 devices in a mesh: span: 8 (over z, y), plane: 4 (over x, core).
Axes of the slice: x: 2, y: 2, z: 4, core: 2. Of those that a mesh axis runs over, the one named last changes fastest.
Arguments:
- adjoint: float32 [3, 32, 81, 512], P(None, 'span', None, 'plane'), may hold values from -6 to 6
- checkpoints: bfloat16 [8, 2, 32, 81, 512], P(None, None, 'span', None, 'plane'), may hold values from -4 to 4
- checkpoint_step: int32 [3], replicated, may hold values from 0 to 7
- metric: float32 [2, 512], P(None, 'plane'), may hold values from 0.004 to 0.016
- helmholtz_inverse: float32 [32, 81, 81], P('span'), may hold values from -0.08 to 0.8
- wall_element: int32 [1024, 2], replicated, may hold values from 0 to 511
- wall_local: int32 [1024, 2], replicated, may hold values from 0 to 80
- wall_weight: float32 [32, 1024], P('span'), may hold values from 0.7 to 140
Outputs:
- adjoint_next: float32 [3, 32, 81, 512], P(None, 'span', None, 'plane')
- control_gradient: float32 [32, 1024], P('span', 'plane')
The draws below stay inside these ranges and needn't reach their ends.
All inputs are finite; a program needn't handle non-finite values.
Results may differ from the reference program's by a relative error of at most 0.00065.
Values may be sent and summed in bfloat16 or wider, within the bound.
A program may use at most 128 MiB of HBM per device.

```python
import math
import jax
import jax.numpy as jnp
import numpy as np
from jax import lax

P_SIZE = 8
Q = 81
NZ = 32
NEL = 512
NWALL = 1024
NCK = 8
NSTEP = 3


def draw_helmholtz_inverse(key, part):
    key_diag = jax.random.fold_in(key, 11)
    key_off = jax.random.fold_in(key, 12)
    diagonal = jnp.exp(jax.random.uniform(key_diag, (NZ, Q), jnp.float32, math.log(0.3), math.log(0.8)))
    spread = jnp.clip(0.02 * jax.random.normal(key_off, (NZ, Q, Q), jnp.float32), -0.08, 0.08)
    unit_matrix = jnp.eye(Q, dtype=jnp.float32)
    return diagonal[:, :, None] * unit_matrix + spread * (1.0 - unit_matrix)


def draw_wall_weight(key, part):
    row_pos = jnp.arange(NZ, dtype=jnp.float32)[:, None] / (NZ - 1)
    col_pos = jnp.arange(NWALL, dtype=jnp.float32)[None, :] / (NWALL - 1)
    exponent = 0.5
    factor = jnp.exp(jax.random.uniform(jax.random.fold_in(key, 21), (NZ, NWALL), jnp.float32, math.log(0.7), math.log(1.4)))
    return factor * jnp.power(10.0, exponent * (row_pos + col_pos))


def touch_ends(drawn, stream_key, smallest, top_value):
    place = [jax.random.randint(jax.random.fold_in(stream_key, axis), (), 0, length) for axis, length in enumerate(drawn.shape)]
    main_axis = drawn.shape.index(max(drawn.shape))
    next_to = place[:main_axis] + [(place[main_axis] + 1) % drawn.shape[main_axis]] + place[main_axis + 1:]
    return drawn.at[tuple(place)].set(smallest).at[tuple(next_to)].set(top_value)


def shard_levels(rng, shape, shards, smallest, top_value):
    loudness = 1.0
    for dim, blocks in shards:
        draws = jax.random.uniform(jax.random.fold_in(jax.random.fold_in(rng, 6), dim), (blocks,), jnp.float32, smallest / len(shards), top_value / len(shards))
        loudness = loudness * jnp.repeat(jnp.exp(draws), shape[dim] // blocks).reshape((-1,) + (1,) * (len(shape) - 1 - dim))
    return loudness


def normal_values(stream_key, shape, scale, reach, split=(), kind=jnp.bfloat16):
    entries = scale * jax.random.normal(stream_key, shape, jnp.float32)
    if split:
        entries = entries * shard_levels(stream_key, shape, split, -0.22, 0.18)
    return jnp.clip(entries, -reach, reach).astype(kind)


def setup_inputs(seed: int = 0) -> dict:
    keys = jax.random.split(jax.random.key(seed), 9)
    adjoint = normal_values(keys[0], (3, NZ, Q, NEL), 1.0, 6.0, ((1, 8), (3, 4)), jnp.float32)
    checkpoints = normal_values(keys[1], (NCK, 2, NZ, Q, NEL), 0.7, 4.0, ((2, 8), (4, 4)))
    checkpoint_step = jax.random.randint(keys[2], (NSTEP,), 0, NCK).astype(jnp.int32)
    metric = jnp.clip(jnp.exp(math.log(0.016) - 1.3862944 * jax.random.uniform(keys[3], (2, NEL), jnp.float32) ** shard_levels(keys[3], (2, NEL), ((1, 4),), -0.2, 0.2)), 0.004, 0.016)
    helmholtz_inverse = draw_helmholtz_inverse(jax.random.fold_in(keys[8], 71), 0)
    wall_element = touch_ends(jax.random.randint(keys[5], (NWALL, 2), 0, NEL), jax.random.fold_in(keys[5], 1), 0, NEL - 1).astype(jnp.int32)
    wall_local = touch_ends(jax.random.randint(keys[6], (NWALL, 2), 0, Q), jax.random.fold_in(keys[6], 1), 0, Q - 1).astype(jnp.int32)
    wall_weight = draw_wall_weight(jax.random.fold_in(keys[8], 71), 0)
    return {"adjoint": adjoint, "checkpoints": checkpoints, "checkpoint_step": checkpoint_step, "metric": metric, "helmholtz_inverse": helmholtz_inverse, "wall_element": wall_element, "wall_local": wall_local, "wall_weight": wall_weight}


HIGHEST = lax.Precision.HIGHEST

def chebyshev_matrix(degree):
    points = np.arange(degree + 1)
    abscissa = np.cos(np.pi * points / degree)
    signed = np.where((points == 0) | (points == degree), 2.0, 1.0) * (-1.0) ** points
    spacing = abscissa[:, None] - abscissa[None, :] + np.eye(degree + 1)
    matrix = signed[:, None] / signed[None, :] / spacing
    return matrix - np.eye(degree + 1) * np.sum(matrix, axis=1)[:, None]

def fourier_table(length):
    row_index = np.arange(length)[:, None]
    column = np.arange(length)[None, :]
    wavenumber = (row_index + 1) // 2
    phase_angle = 2.0 * np.pi * wavenumber * column / length
    parity = row_index % 2
    base_rows = np.where(row_index == 0, 1.0, np.where(parity == 1, np.cos(phase_angle), np.sin(phase_angle)))
    row_scale = np.where((row_index == 0) | (row_index == length - 1), 1.0 / np.sqrt(length), np.sqrt(2.0 / length))
    return base_rows * row_scale

def transport(field_data, velocity, metric):
    side_nodes = P_SIZE + 1
    matrix = jnp.asarray(chebyshev_matrix(P_SIZE), jnp.float32)
    shaped = field_data.reshape(field_data.shape[0], field_data.shape[1], side_nodes, side_nodes, field_data.shape[3])
    first_dir = jnp.einsum('ai,czibe->czabe', matrix, shaped, precision=HIGHEST).reshape(field_data.shape)
    second_dir = jnp.einsum('bi,czaie->czabe', matrix, shaped, precision=HIGHEST).reshape(field_data.shape)
    speed_data = velocity.astype(jnp.float32)
    return field_data + speed_data[0] * (metric[0] * first_dir) + speed_data[1] * (metric[1] * second_dir)

def one_component(component, velocity, metric, helmholtz_inverse):
    advected = transport(component[None], velocity, metric)[0]
    basis_table = jnp.asarray(fourier_table(NZ), jnp.float32)
    coefficients = jnp.einsum('jz,zqe->jqe', basis_table, advected, precision=HIGHEST)
    solved = jnp.einsum('jqr,jre->jqe', helmholtz_inverse, coefficients, precision=HIGHEST)
    return jnp.einsum('jz,jqe->zqe', basis_table, solved, precision=HIGHEST)

def reference(adjoint, checkpoints, checkpoint_step, metric, helmholtz_inverse, wall_element, wall_local, wall_weight):
    gradient_sum = jnp.zeros((NZ, NWALL), jnp.float32)
    for substep in range(NSTEP):
        slot_index = checkpoint_step[substep]
        velocity = lax.dynamic_index_in_dim(checkpoints, slot_index, 0, keepdims=False)
        adjoint = lax.map(lambda component: one_component(component, velocity, metric, helmholtz_inverse), adjoint)
        values = adjoint[1][:, wall_local, wall_element]
        speeds = velocity[1][:, wall_local, wall_element].astype(jnp.float32)
        gradient_sum = gradient_sum + lax.optimization_barrier(jnp.sum(values * speeds, axis=2))
    weighted = wall_weight * gradient_sum
    inverse_rms = lax.rsqrt(jnp.mean(weighted * weighted) + 1e-06)
    return (adjoint, weighted * inverse_rms)
```

```python
import jax
import jax.numpy as jnp
import numpy as np
from jax import lax
from jax.sharding import PartitionSpec as P

P_SIZE = 8
NSTEP = 3


HIGHEST = lax.Precision.HIGHEST


def chebyshev_matrix(degree):
    points = np.arange(degree + 1)
    abscissa = np.cos(np.pi * points / degree)
    signed = np.where((points == 0) | (points == degree), 2.0, 1.0) * (-1.0) ** points
    spacing = abscissa[:, None] - abscissa[None, :] + np.eye(degree + 1)
    matrix = signed[:, None] / signed[None, :] / spacing
    return matrix - np.eye(degree + 1) * np.sum(matrix, axis=1)[:, None]


def fourier_table(length):
    row_index = np.arange(length)[:, None]
    column = np.arange(length)[None, :]
    wavenumber = (row_index + 1) // 2
    phase_angle = 2.0 * np.pi * wavenumber * column / length
    parity = row_index % 2
    base_rows = np.where(
        row_index == 0, 1.0, np.where(parity == 1, np.cos(phase_angle), np.sin(phase_angle))
    )
    row_scale = np.where(
        (row_index == 0) | (row_index == length - 1), 1.0 / np.sqrt(length), np.sqrt(2.0 / length)
    )
    return base_rows * row_scale


def transport(field_data, velocity, metric):
    side_nodes = P_SIZE + 1
    matrix = jnp.asarray(chebyshev_matrix(P_SIZE), jnp.float32)
    shaped = field_data.reshape(
        field_data.shape[0], field_data.shape[1], side_nodes, side_nodes, field_data.shape[3]
    )
    first_dir = jnp.einsum("ai,czibe->czabe", matrix, shaped, precision=HIGHEST).reshape(
        field_data.shape
    )
    second_dir = jnp.einsum("bi,czaie->czabe", matrix, shaped, precision=HIGHEST).reshape(
        field_data.shape
    )
    speed_data = velocity.astype(jnp.float32)
    return (
        field_data
        + speed_data[0] * (metric[0] * first_dir)
        + speed_data[1] * (metric[1] * second_dir)
    )


def forward_modes(gathered):
    basis_table = jnp.asarray(fourier_table(gathered.shape[1]), jnp.float32)
    return jnp.einsum("jz,czqe->cjqe", basis_table, gathered, precision=HIGHEST)


def backward_planes(solved):
    basis_table = jnp.asarray(fourier_table(solved.shape[1]), jnp.float32)
    return jnp.einsum("jz,cjqe->czqe", basis_table, solved, precision=HIGHEST)


def solve_modes(inverse_block, coefficients):
    return jnp.einsum("jqr,cjre->cjqe", inverse_block, coefficients, precision=HIGHEST)


def to_plane_layout(point_data):
    return lax.all_to_all(point_data, "span", split_axis=1, concat_axis=3, tiled=True)


def wall_terms(field_one, speed_one, flat_index, inside, wall_count):
    rows = field_one.shape[0]
    values = jnp.take(field_one.reshape(rows, -1), flat_index, axis=1)
    speeds = jnp.take(speed_one.reshape(rows, -1), flat_index, axis=1).astype(jnp.float32)
    product = jnp.where(inside, values * speeds, 0.0).reshape(rows, wall_count, 2)
    return jnp.sum(product, axis=2)


def on_device(
    adjoint,
    checkpoints,
    checkpoint_step,
    metric,
    helmholtz_inverse,
    wall_element,
    wall_local,
    wall_weight,
):
    planes_dev = adjoint.shape[1]
    elems_dev = adjoint.shape[3]
    wall_count = wall_element.shape[0]
    span_count = lax.axis_size("span")
    share = elems_dev // span_count
    all_modes = lax.all_gather(helmholtz_inverse, "span", axis=0, tiled=True)
    offset = lax.axis_index("plane") * elems_dev
    local_element = wall_element - offset
    inside = ((local_element >= 0) & (local_element < elems_dev)).reshape(-1)
    flat_index = (wall_local * elems_dev + jnp.clip(local_element, 0, elems_dev - 1)).reshape(-1)
    velocity = jnp.stack([
        lax.dynamic_index_in_dim(checkpoints, checkpoint_step[s], 0, keepdims=False)
        for s in range(NSTEP)
    ])
    velocity = lax.all_to_all(velocity, "span", split_axis=4, concat_axis=2, tiled=True)
    field = lax.all_to_all(adjoint, "span", split_axis=3, concat_axis=1, tiled=True)
    scale = lax.dynamic_slice_in_dim(metric, lax.axis_index("span") * share, share, 1)
    product = 0.0
    for substep in range(NSTEP):
        advected = transport(field, velocity[substep], scale)
        field = backward_planes(solve_modes(all_modes, forward_modes(advected)))
        product = product + field[1] * velocity[substep, 1].astype(jnp.float32)
    both = to_plane_layout(jnp.concatenate([field, product[None]], axis=0))
    gathered = jnp.take(both[3].reshape(planes_dev, -1), flat_index, axis=1)
    partial_sum = jnp.where(inside, gathered, 0.0).reshape(planes_dev, wall_count, 2).sum(axis=2)
    weighted = wall_weight * partial_sum
    grad_share = lax.psum_scatter(weighted, "plane", scatter_dimension=1, tiled=True)
    square_total = lax.psum(jnp.sum(grad_share * grad_share), ("span", "plane"))
    inverse_rms = lax.rsqrt(square_total / (planes_dev * span_count * wall_count) + 1e-06)
    return (both[:3], grad_share * inverse_rms)


def solution(mesh):
    placed = (
        P(None, "span", None, "plane"),
        P(None, None, "span", None, "plane"),
        P(),
        P(None, "plane"),
        P("span", None, None),
        P(),
        P(),
        P("span", None),
    )
    return jax.shard_map(
        on_device,
        mesh=mesh,
        in_specs=placed,
        out_specs=(P(None, "span", None, "plane"), P("span", "plane")),
        check_vma=False,
    )
```

```python
import functools

import jax
import jax.numpy as jnp
import ml_dtypes
import numpy as np
from jax import lax
from jax.experimental import pallas as pl
from jax.experimental.pallas import tpu as pltpu
from jax.sharding import PartitionSpec as P

P_SIZE = 8
NSTEP = 3


HIGHEST = lax.Precision.HIGHEST


def chebyshev_matrix(degree):
    points = np.arange(degree + 1)
    abscissa = np.cos(np.pi * points / degree)
    signed = np.where((points == 0) | (points == degree), 2.0, 1.0) * (-1.0) ** points
    spacing = abscissa[:, None] - abscissa[None, :] + np.eye(degree + 1)
    matrix = signed[:, None] / signed[None, :] / spacing
    return matrix - np.eye(degree + 1) * np.sum(matrix, axis=1)[:, None]


def fourier_table(length):
    row_index = np.arange(length)[:, None]
    column = np.arange(length)[None, :]
    wavenumber = (row_index + 1) // 2
    phase_angle = 2.0 * np.pi * wavenumber * column / length
    parity = row_index % 2
    base_rows = np.where(
        row_index == 0, 1.0, np.where(parity == 1, np.cos(phase_angle), np.sin(phase_angle))
    )
    row_scale = np.where(
        (row_index == 0) | (row_index == length - 1), 1.0 / np.sqrt(length), np.sqrt(2.0 / length)
    )
    return base_rows * row_scale


def transport(field_data, velocity, metric):
    side_nodes = P_SIZE + 1
    matrix = jnp.asarray(chebyshev_matrix(P_SIZE), jnp.float32)
    shaped = field_data.reshape(
        field_data.shape[0], field_data.shape[1], side_nodes, side_nodes, field_data.shape[3]
    )
    first_dir = jnp.einsum("ai,czibe->czabe", matrix, shaped, precision=HIGHEST).reshape(
        field_data.shape
    )
    second_dir = jnp.einsum("bi,czaie->czabe", matrix, shaped, precision=HIGHEST).reshape(
        field_data.shape
    )
    speed_data = velocity.astype(jnp.float32)
    return (
        field_data
        + speed_data[0] * (metric[0] * first_dir)
        + speed_data[1] * (metric[1] * second_dir)
    )


def forward_modes(gathered):
    basis_table = jnp.asarray(fourier_table(gathered.shape[1]), jnp.float32)
    return jnp.einsum("jz,czqe->cjqe", basis_table, gathered, precision=HIGHEST)


def backward_planes(solved):
    basis_table = jnp.asarray(fourier_table(solved.shape[1]), jnp.float32)
    return jnp.einsum("jz,cjqe->czqe", basis_table, solved, precision=HIGHEST)


def solve_modes(inverse_block, coefficients):
    return jnp.einsum("jqr,cjre->cjqe", inverse_block, coefficients, precision=HIGHEST)


def to_plane_layout(point_data):
    return lax.all_to_all(point_data, "span", split_axis=1, concat_axis=3, tiled=True)


def wall_terms(field_one, speed_one, flat_index, inside, wall_count):
    rows = field_one.shape[0]
    values = jnp.take(field_one.reshape(rows, -1), flat_index, axis=1)
    speeds = jnp.take(speed_one.reshape(rows, -1), flat_index, axis=1).astype(jnp.float32)
    product = jnp.where(inside, values * speeds, 0.0).reshape(rows, wall_count, 2)
    return jnp.sum(product, axis=2)


def on_device(
    adjoint,
    checkpoints,
    checkpoint_step,
    metric,
    helmholtz_inverse,
    wall_element,
    wall_local,
    wall_weight,
):
    planes_dev = adjoint.shape[1]
    elems_dev = adjoint.shape[3]
    wall_count = wall_element.shape[0]
    span_count = lax.axis_size("span")
    share = elems_dev // span_count
    all_modes = lax.all_gather(helmholtz_inverse, "span", axis=0, tiled=True)
    offset = lax.axis_index("plane") * elems_dev
    local_element = wall_element - offset
    inside = ((local_element >= 0) & (local_element < elems_dev)).reshape(-1)
    flat_index = (wall_local * elems_dev + jnp.clip(local_element, 0, elems_dev - 1)).reshape(-1)
    velocity = jnp.stack([
        lax.dynamic_index_in_dim(checkpoints, checkpoint_step[s], 0, keepdims=False)
        for s in range(NSTEP)
    ])
    velocity = lax.all_to_all(velocity, "span", split_axis=4, concat_axis=2, tiled=True)
    field = lax.all_to_all(adjoint, "span", split_axis=3, concat_axis=1, tiled=True)
    scale = lax.dynamic_slice_in_dim(metric, lax.axis_index("span") * share, share, 1)
    product = 0.0
    for substep in range(NSTEP):
        advected = transport(field, velocity[substep], scale)
        field = backward_planes(solve_modes(all_modes, forward_modes(advected)))
        product = product + field[1] * velocity[substep, 1].astype(jnp.float32)
    both = to_plane_layout(jnp.concatenate([field, product[None]], axis=0))
    gathered = jnp.take(both[3].reshape(planes_dev, -1), flat_index, axis=1)
    partial_sum = jnp.where(inside, gathered, 0.0).reshape(planes_dev, wall_count, 2).sum(axis=2)
    weighted = wall_weight * partial_sum
    grad_share = lax.psum_scatter(weighted, "plane", scatter_dimension=1, tiled=True)
    square_total = lax.psum(jnp.sum(grad_share * grad_share), ("span", "plane"))
    inverse_rms = lax.rsqrt(square_total / (planes_dev * span_count * wall_count) + 1e-06)
    return (both[:3], grad_share * inverse_rms)


MESH = pl.DeviceIdType.MESH
F32 = jnp.float32
BF16 = jnp.bfloat16
LANES = 128


def swap_blocks(parts, share):
    count = len(parts)
    width = count * share
    lane = lax.broadcasted_iota(jnp.int32, parts[0].shape, 1)
    k = count // 2
    while k:
        upper = (lane // (k * share)) % 2 == 1
        new = list(parts)
        for i in range(count):
            if (i // k) % 2 == 0:
                a, b = parts[i], parts[i + k]
                new[i] = jnp.where(upper, pltpu.roll(b, k * share, 1), a)
                new[i + k] = jnp.where(upper, b, pltpu.roll(a, width - k * share, 1))
        parts = new
        k //= 2
    return parts


def greet(spans, planes):
    me, p = lax.axis_index("span"), lax.axis_index("plane")
    barrier = pltpu.get_barrier_semaphore()
    for o in range(1, spans):
        pl.semaphore_signal(barrier, 1, device_id={"span": (me + o) % spans}, device_id_type=MESH)
    for o in range(1, planes):
        pl.semaphore_signal(barrier, 1, device_id={"plane": (p + o) % planes}, device_id_type=MESH)
    pl.semaphore_wait(barrier, spans + planes - 2)


def remote(src, dst, sems, kind, o, target):
    return pltpu.make_async_remote_copy(
        src_ref=src, dst_ref=dst, send_sem=sems.at[0, kind, o], recv_sem=sems.at[1, kind, o],
        device_id=target, device_id_type=MESH,
    )


def enter_kernel(spans, planes, zdev, q, qp,
                 step_ref, adj_ref, ck_ref, inv_ref,
                 xs_ref, vs_ref, modes_ref,
                 tail, snd, rcv, vsnd, vrcv, sems, local_sem):
    share = LANES // spans
    me, p = lax.axis_index("span"), lax.axis_index("plane")
    bulk = q - 1
    half = bulk // 2
    slabs = 3 * zdev
    sets = 2 * slabs // spans
    greet(spans, planes)

    def span_to(o):
        return {"span": (me + o) % spans}

    xpeer = {"plane": (p + 2) % planes}
    cpeer = {"plane": p + 1 - 2 * (p % 2)}
    px = (p + 2) % planes
    pc = p + 1 - 2 * (p % 2)
    pcx = (pc + 2) % planes
    stage1, stage2x, stage2c, stage3 = [], [], [], []
    for o in range(1, spans):
        s = (me + spans - o) % spans
        out = remote(inv_ref.at[p], modes_ref.at[p, me], sems, 0, o, span_to(o))
        out.start()
        stage1.append((out, remote(inv_ref.at[p], modes_ref.at[p, s], sems, 0, o, span_to(o))))
        stage2x.append((remote(modes_ref.at[p, s], modes_ref.at[p, s], sems, 1, o, xpeer),
                        remote(modes_ref.at[p, s], modes_ref.at[px, s], sems, 1, o, xpeer)))
        stage2c.append((remote(modes_ref.at[p, s], modes_ref.at[p, s], sems, 2, o, cpeer),
                        remote(modes_ref.at[p, s], modes_ref.at[pc, s], sems, 2, o, cpeer)))
        stage3.append((remote(modes_ref.at[px, s], modes_ref.at[px, s], sems, 3, o, cpeer),
                       remote(modes_ref.at[px, s], modes_ref.at[pcx, s], sems, 3, o, cpeer)))

    tail[...] = jnp.zeros_like(tail)
    for k in range(slabs):
        tail[k % spans, k // spans:k // spans + 1, :] = adj_ref[k // zdev, k % zdev, bulk:q, :]
    for t in range(NSTEP):
        slot = step_ref[t]
        for k in range(2 * zdev):
            row = ck_ref[slot, k // zdev, k % zdev].astype(F32)[bulk:q, :]
            tail[k, 2 + t:3 + t, :] = row
    for i in range(sets):
        parts = []
        for g in range(spans):
            h = spans * i + g
            k, r = h // 2, (h % 2) * half
            parts.append(adj_ref[k // zdev, k % zdev, r:r + half, :])
        parts = swap_blocks(parts, share)
        for d in range(spans):
            snd[d, i * half:(i + 1) * half, :] = parts[d]
    parts = swap_blocks([tail[g] for g in range(spans)], share)
    for d in range(spans):
        snd[d, sets * half:, :] = parts[d]
    fields, speeds = [], []
    for o in range(1, spans):
        to, s = (me + o) % spans, (me + spans - o) % spans
        out = remote(snd.at[to], rcv.at[me], sems, 4, o, span_to(o))
        out.start()
        fields.append((out, remote(snd.at[to], rcv.at[s], sems, 4, o, span_to(o))))
    own = pltpu.make_async_copy(snd.at[me], rcv.at[me], local_sem.at[0])
    own.start()
    for t in range(NSTEP):
        slot = step_ref[t]
        parts = [ck_ref[slot, k // zdev, k % zdev].astype(F32)[:bulk] for k in range(2 * zdev)]
        parts = swap_blocks(parts, share)
        for d in range(spans):
            vsnd[d, t] = parts[d].astype(BF16)
    for o in range(1, spans):
        to, s = (me + o) % spans, (me + spans - o) % spans
        out = remote(vsnd.at[to], vrcv.at[me], sems, 5, o, span_to(o))
        out.start()
        speeds.append((out, remote(vsnd.at[to], vrcv.at[s], sems, 5, o, span_to(o))))
    vown = pltpu.make_async_copy(vsnd.at[me], vrcv.at[me], local_sem.at[1])
    vown.start()
    mine = [pltpu.make_async_copy(inv_ref.at[j], modes_ref.at[j, me], local_sem.at[2 + j])
            for j in range(zdev)]
    for c in mine:
        c.start()
    xs_ref[bulk:, :] = jnp.zeros_like(xs_ref[bulk:, :])
    vs_ref[:, :, bulk:, :] = jnp.zeros_like(vs_ref[:, :, bulk:, :])

    for o in range(spans - 1):
        stage1[o][1].wait_recv()
        stage2x[o][0].start()
        stage2c[o][0].start()
    for o in range(spans - 1):
        stage2x[o][1].wait_recv()
        stage3[o][0].start()
    own.wait()
    for c in fields:
        c[1].wait_recv()
    for i in range(sets):
        parts = swap_blocks([rcv[s, i * half:(i + 1) * half, :] for s in range(spans)], share)
        for g in range(spans):
            h = spans * i + g
            k, r = h // 2, (h % 2) * half
            xs_ref[r:r + half, k * LANES:(k + 1) * LANES] = parts[g]
    parts = swap_blocks([rcv[s, sets * half:, :] for s in range(spans)], share)
    for k in range(slabs):
        xs_ref[bulk:q, k * LANES:(k + 1) * LANES] = parts[k % spans][k // spans:k // spans + 1]
    for t in range(NSTEP):
        for k in range(2 * zdev):
            z = k % zdev
            vs_ref[t, k // zdev, bulk:q, z * LANES:(z + 1) * LANES] = parts[k][2 + t:3 + t]
    vown.wait()
    for c in speeds:
        c[1].wait_recv()
    for t in range(NSTEP):
        parts = swap_blocks([vrcv[s, t].astype(F32) for s in range(spans)], share)
        for k in range(2 * zdev):
            z = k % zdev
            vs_ref[t, k // zdev, :bulk, z * LANES:(z + 1) * LANES] = parts[k]
    for c in mine:
        c.wait()
    for group in (stage2c, stage3):
        for c in group:
            c[1].wait_recv()
    for group in (stage1, stage2x, stage2c, stage3, fields, speeds):
        for c in group:
            c[0].wait_send()


def split(x):
    high = x.astype(BF16)
    return high, (x - high.astype(F32)).astype(BF16)


def mul3(a, b, dims=((1,), (0,))):
    def one(x, y):
        return lax.dot_general(x, y, (dims, ((), ())), preferred_element_type=F32)
    return one(a[0], b[0]) + (one(a[0], b[1]) + one(a[1], b[0]))


def steps_kernel(spans, planes, zdev, qp,
                 xs_ref, vs_ref, modes_ref, metric_ref, elem_ref, local_ref,
                 basis_ref, diff_ref, place_ref,
                 out_ref, wall_ref,
                 field, coef, solved, product, modes_hi, modes_lo):
    share = LANES // spans
    wide = zdev * LANES
    me, p = lax.axis_index("span"), lax.axis_index("plane")
    lane = lax.broadcasted_iota(jnp.int32, (1, LANES), 1)
    rolled = pltpu.roll(metric_ref[...], (LANES - me * share) % LANES, 1)
    scale = jnp.where(lane < share, rolled, 0.0)
    k = share
    while k < LANES:
        scale = scale + pltpu.roll(scale, k, 1)
        k *= 2
    for j in range(zdev):
        for s in range(spans):
            high, low = split(modes_ref[j, s])
            modes_hi[j, s * qp:(s + 1) * qp, :] = high
            modes_lo[j, s * qp:(s + 1) * qp, :] = low
    field[...] = xs_ref[...]
    product[...] = jnp.zeros_like(product)
    block = lax.broadcasted_iota(jnp.int32, (1, 3 * LANES), 1) % LANES // share
    first = jnp.concatenate([scale[0:1]] * zdev, axis=1)
    second = jnp.concatenate([scale[1:2]] * zdev, axis=1)

    def one_step(t, carry):
        v0 = vs_ref[t, 0] * first
        v1 = vs_ref[t, 1] * second
        for c in range(3):
            x = field[:, c * wide:(c + 1) * wide]
            d = mul3((diff_ref[0], diff_ref[1]), split(x))
            coef[c * qp:(c + 1) * qp, :] = x + v0 * d[:qp] + v1 * d[qp:]
        y = mul3(split(coef[...]), (basis_ref[0], basis_ref[1]))
        coef[...] = y
        for j in range(zdev):
            lanes = slice(j * LANES, (j + 1) * LANES)
            x = jnp.concatenate([coef[c * qp:(c + 1) * qp, lanes] for c in range(3)], axis=1)
            r = mul3((modes_hi[j, :, :qp], modes_lo[j, :, :qp]), split(x))
            total = r[:qp]
            for s in range(1, spans):
                total = jnp.where(block == s, r[s * qp:(s + 1) * qp], total)
            for c in range(3):
                solved[c * qp:(c + 1) * qp, lanes] = total[:, c * LANES:(c + 1) * LANES]
        y = mul3(split(solved[...]), (basis_ref[0], basis_ref[1]), ((1,), (1,)))
        for c in range(3):
            field[:, c * wide:(c + 1) * wide] = y[c * qp:(c + 1) * qp]
        product[...] += y[qp:2 * qp] * vs_ref[t, 1]
        return carry

    lax.fori_loop(0, NSTEP, one_step, 0)
    out_ref[...] = field[...]

    high, low = split(product[...])
    base = p * LANES + me * share
    mode = lax.broadcasted_iota(jnp.int32, (1, qp), 1)
    near = lane % share

    def picked(row):
        total = 0.0
        for k in range(2):
            pick = jnp.where(local_ref[pl.ds(row, LANES), k:k + 1] == mode, 1.0, 0.0).astype(BF16)
            keep = elem_ref[pl.ds(row, LANES), k:k + 1] - base == near
            keep = jnp.concatenate([jnp.where(keep, 1.0, 0.0)] * zdev, axis=1)
            got = jnp.dot(pick, high, preferred_element_type=F32)
            got = got + jnp.dot(pick, low, preferred_element_type=F32)
            total = total + got * keep
        return split(total)

    for part in range(planes):
        total = 0.0
        for h in range(2):
            pair = picked((part * 2 + h) * LANES)
            for v in pair:
                total = total + lax.dot_general(
                    place_ref[h], v, (((1,), (1,)), ((), ())), preferred_element_type=F32)
        for s in range(spans):
            wall_ref[s, part] = total[s * 8:(s + 1) * 8]


def leave_kernel(spans, planes, zdev, q, count,
                 xs_ref, wall_ref, weight_ref,
                 out_ref, grad_ref,
                 tail, snd, rcv, wrcv, part, prcv, square, srcv, total, trcv, sems, local_sem):
    share = LANES // spans
    me, p = lax.axis_index("span"), lax.axis_index("plane")
    bulk = q - 1
    half = bulk // 2
    slabs = 3 * zdev
    sets = 2 * slabs // spans
    greet(spans, planes)

    def exchange(kind, size, axis, pick_src, dst):
        at = lax.axis_index(axis)
        pairs = []
        for o in range(1, size):
            to, s = (at + o) % size, (at + size - o) % size
            out = remote(pick_src(to), dst.at[at], sems, kind, o, {axis: to})
            out.start()
            pairs.append((out, remote(pick_src(to), dst.at[s], sems, kind, o, {axis: to})))
        return pairs

    walls = exchange(0, spans, "span", lambda to: wall_ref.at[to], wrcv)
    wown = pltpu.make_async_copy(wall_ref.at[me], wrcv.at[me], local_sem.at[0])
    wown.start()
    tail[...] = jnp.zeros_like(tail)
    for k in range(slabs):
        tail[k % spans, k // spans:k // spans + 1, :] = xs_ref[bulk:q, k * LANES:(k + 1) * LANES]
    for i in range(sets):
        parts = []
        for g in range(spans):
            h = spans * i + g
            k, r = h // 2, (h % 2) * half
            parts.append(xs_ref[r:r + half, k * LANES:(k + 1) * LANES])
        parts = swap_blocks(parts, share)
        for d in range(spans):
            snd[d, i * half:(i + 1) * half, :] = parts[d]
    parts = swap_blocks([tail[g] for g in range(spans)], share)
    for d in range(spans):
        snd[d, sets * half:, :] = parts[d]
    fields = exchange(1, spans, "span", lambda to: snd.at[to], rcv)
    own = pltpu.make_async_copy(snd.at[me], rcv.at[me], local_sem.at[1])
    own.start()

    wown.wait()
    for c in walls:
        c[1].wait_recv()
    part[...] = sum(wrcv[s] for s in range(spans))
    rows = exchange(2, planes, "plane", lambda to: part.at[to], prcv)
    pown = pltpu.make_async_copy(part.at[p], prcv.at[p], local_sem.at[2])
    pown.start()
    pown.wait()
    for c in rows:
        c[1].wait_recv()
    block = sum(prcv[s] for s in range(planes))
    sums = jnp.concatenate([block[:zdev], block[zdev:]], axis=1)
    weight = weight_ref[:, pl.ds(pl.multiple_of(p * 2 * LANES, 2 * LANES), 2 * LANES)]
    weighted = weight * sums
    sq = weighted * weighted
    square[...] = jnp.broadcast_to(jnp.sum(sq[:, :LANES] + sq[:, LANES:], axis=0, keepdims=True), (8, LANES))
    squares = exchange(3, spans, "span", lambda to: square, srcv)
    srcv[me] = square[...]
    for c in squares:
        c[1].wait_recv()
    total[...] = sum(srcv[s] for s in range(spans))
    totals = exchange(4, planes, "plane", lambda to: total, trcv)
    trcv[p] = total[...]
    for c in totals:
        c[1].wait_recv()
    full = jnp.sum(sum(trcv[s] for s in range(planes))[0:1], axis=1, keepdims=True)
    grad_ref[...] = weighted * lax.rsqrt(full / count + 1e-06)

    own.wait()
    for c in fields:
        c[1].wait_recv()
    for i in range(sets):
        parts = swap_blocks([rcv[s, i * half:(i + 1) * half, :] for s in range(spans)], share)
        for g in range(spans):
            h = spans * i + g
            k, r = h // 2, (h % 2) * half
            out_ref[k // zdev, k % zdev, r:r + half, :] = parts[g]
    parts = swap_blocks([rcv[s, sets * half:, :] for s in range(spans)], share)
    for k in range(slabs):
        out_ref[k // zdev, k % zdev, bulk:q, :] = parts[k % spans][k // spans:k // spans + 1]
    for group in (walls, fields, rows, squares, totals):
        for c in group:
            c[0].wait_send()


def halves(table):
    high = table.astype(np.float32).astype(ml_dtypes.bfloat16)
    low = (table - high.astype(np.float64)).astype(np.float32).astype(ml_dtypes.bfloat16)
    return np.stack([high, low])


def tables(spans, zdev, q, qp):
    share = LANES // spans
    fourier = fourier_table(spans * zdev)
    order = np.array([s * zdev + z for z in range(zdev) for s in range(spans)])
    basis = np.kron(fourier[order][:, order].T, np.eye(share))
    side = P_SIZE + 1
    matrix = chebyshev_matrix(P_SIZE)
    diff = np.zeros((2 * qp, qp))
    diff[:q, :q] = np.kron(matrix, np.eye(side))
    diff[qp:qp + q, :q] = np.kron(np.eye(side), matrix)
    place = np.zeros((2, spans * 8, zdev * LANES), ml_dtypes.bfloat16)
    for h in range(2):
        for s in range(spans):
            for z in range(zdev):
                at = z * LANES + s * share
                place[h, s * 8 + h * zdev + z, at:at + share] = 1.0
    return halves(basis), halves(diff), place


def vmem(n):
    return [pl.BlockSpec(memory_space=pltpu.VMEM)] * n


def kernels_on_device(spans, planes, adjoint, checkpoints, checkpoint_step, metric,
                      helmholtz_inverse, wall_element, wall_local, wall_weight):
    _, zdev, q, _ = adjoint.shape
    wall_count = wall_element.shape[0]
    qp = -(-q // 16) * 16
    bulk, wide = q - 1, zdev * LANES
    rows = 3 * zdev * bulk // spans + 8
    inverse = jnp.pad(helmholtz_inverse, ((0, 0), (0, qp - q), (0, LANES - q)))
    shape = jax.ShapeDtypeStruct
    field, speed, modes = pl.pallas_call(
        functools.partial(enter_kernel, spans, planes, zdev, q, qp),
        out_shape=(shape((qp, 3 * wide), F32), shape((NSTEP, 2, qp, wide), F32),
                   shape((zdev, spans, qp, LANES), F32)),
        in_specs=[pl.BlockSpec(memory_space=pltpu.SMEM)] + vmem(3),
        out_specs=tuple(vmem(3)),
        scratch_shapes=[
            pltpu.VMEM((spans, 8, LANES), F32),
            pltpu.VMEM((spans, rows, LANES), F32),
            pltpu.VMEM((spans, rows, LANES), F32),
            pltpu.VMEM((spans, NSTEP, bulk, LANES), BF16),
            pltpu.VMEM((spans, NSTEP, bulk, LANES), BF16),
            pltpu.SemaphoreType.DMA((2, 6, spans)),
            pltpu.SemaphoreType.DMA((2 + zdev,)),
        ],
        compiler_params=pltpu.CompilerParams(collective_id=0, has_side_effects=True),
        name="enter",
    )(checkpoint_step, adjoint, checkpoints, inverse)
    basis, diff, place = tables(spans, zdev, q, qp)
    field, walls = pl.pallas_call(
        functools.partial(steps_kernel, spans, planes, zdev, qp),
        out_shape=(shape((qp, 3 * wide), F32), shape((spans, planes, 8, LANES), F32)),
        in_specs=vmem(9),
        out_specs=tuple(vmem(2)),
        scratch_shapes=[
            pltpu.VMEM((qp, 3 * wide), F32),
            pltpu.VMEM((3 * qp, wide), F32),
            pltpu.VMEM((3 * qp, wide), F32),
            pltpu.VMEM((qp, wide), F32),
            pltpu.VMEM((zdev, spans * qp, LANES), BF16),
            pltpu.VMEM((zdev, spans * qp, LANES), BF16),
        ],
        name="steps",
    )(field, speed, modes, metric, wall_element, wall_local, basis, diff, place)
    return pl.pallas_call(
        functools.partial(leave_kernel, spans, planes, zdev, q, float(spans * zdev * wall_count)),
        out_shape=(shape(adjoint.shape, F32), shape((zdev, wall_count // planes), F32)),
        in_specs=vmem(3),
        out_specs=tuple(vmem(2)),
        scratch_shapes=[
            pltpu.VMEM((spans, 8, LANES), F32),
            pltpu.VMEM((spans, rows, LANES), F32),
            pltpu.VMEM((spans, rows, LANES), F32),
            pltpu.VMEM((spans, planes, 8, LANES), F32),
            pltpu.VMEM((planes, 8, LANES), F32),
            pltpu.VMEM((planes, 8, LANES), F32),
            pltpu.VMEM((8, LANES), F32),
            pltpu.VMEM((spans, 8, LANES), F32),
            pltpu.VMEM((8, LANES), F32),
            pltpu.VMEM((planes, 8, LANES), F32),
            pltpu.SemaphoreType.DMA((2, 5, spans)),
            pltpu.SemaphoreType.DMA((3,)),
        ],
        compiler_params=pltpu.CompilerParams(collective_id=1, has_side_effects=True),
        name="leave",
    )(field, walls, wall_weight)


def chosen(spans, planes, *args):
    zdev, q, elems = args[0].shape[1:]
    walls = args[5].shape[0]
    fits = (
        elems == LANES and spans == 2 * zdev and planes == zdev == 4
        and walls == planes * 2 * LANES and q % 16 == 1 and q < LANES
    )
    if fits:
        return kernels_on_device(spans, planes, *args)
    return on_device(*args)


def solution(mesh):
    placed = (
        P(None, "span", None, "plane"),
        P(None, None, "span", None, "plane"),
        P(),
        P(None, "plane"),
        P("span", None, None),
        P(),
        P(),
        P("span", None),
    )
    return jax.shard_map(
        functools.partial(chosen, mesh.shape["span"], mesh.shape["plane"]),
        mesh=mesh,
        in_specs=placed,
        out_specs=(P(None, "span", None, "plane"), P("span", "plane")),
        check_vma=False,
    )
```

```python
import functools

import jax
import jax.numpy as jnp
import ml_dtypes
import numpy as np
from jax import lax
from jax.experimental import pallas as pl
from jax.experimental.pallas import tpu as pltpu
from jax.sharding import PartitionSpec as P

P_SIZE = 8
NSTEP = 3


HIGHEST = lax.Precision.HIGHEST


def chebyshev_matrix(degree):
    points = np.arange(degree + 1)
    abscissa = np.cos(np.pi * points / degree)
    signed = np.where((points == 0) | (points == degree), 2.0, 1.0) * (-1.0) ** points
    spacing = abscissa[:, None] - abscissa[None, :] + np.eye(degree + 1)
    matrix = signed[:, None] / signed[None, :] / spacing
    return matrix - np.eye(degree + 1) * np.sum(matrix, axis=1)[:, None]


def fourier_table(length):
    row_index = np.arange(length)[:, None]
    column = np.arange(length)[None, :]
    wavenumber = (row_index + 1) // 2
    phase_angle = 2.0 * np.pi * wavenumber * column / length
    parity = row_index % 2
    base_rows = np.where(
        row_index == 0, 1.0, np.where(parity == 1, np.cos(phase_angle), np.sin(phase_angle))
    )
    row_scale = np.where(
        (row_index == 0) | (row_index == length - 1), 1.0 / np.sqrt(length), np.sqrt(2.0 / length)
    )
    return base_rows * row_scale


def transport(field_data, velocity, metric):
    side_nodes = P_SIZE + 1
    matrix = jnp.asarray(chebyshev_matrix(P_SIZE), jnp.float32)
    shaped = field_data.reshape(
        field_data.shape[0], field_data.shape[1], side_nodes, side_nodes, field_data.shape[3]
    )
    first_dir = jnp.einsum("ai,czibe->czabe", matrix, shaped, precision=HIGHEST).reshape(
        field_data.shape
    )
    second_dir = jnp.einsum("bi,czaie->czabe", matrix, shaped, precision=HIGHEST).reshape(
        field_data.shape
    )
    speed_data = velocity.astype(jnp.float32)
    return (
        field_data
        + speed_data[0] * (metric[0] * first_dir)
        + speed_data[1] * (metric[1] * second_dir)
    )


def forward_modes(gathered):
    basis_table = jnp.asarray(fourier_table(gathered.shape[1]), jnp.float32)
    return jnp.einsum("jz,czqe->cjqe", basis_table, gathered, precision=HIGHEST)


def backward_planes(solved):
    basis_table = jnp.asarray(fourier_table(solved.shape[1]), jnp.float32)
    return jnp.einsum("jz,cjqe->czqe", basis_table, solved, precision=HIGHEST)


def solve_modes(inverse_block, coefficients):
    return jnp.einsum("jqr,cjre->cjqe", inverse_block, coefficients, precision=HIGHEST)


def to_plane_layout(point_data):
    return lax.all_to_all(point_data, "span", split_axis=1, concat_axis=3, tiled=True)


def wall_terms(field_one, speed_one, flat_index, inside, wall_count):
    rows = field_one.shape[0]
    values = jnp.take(field_one.reshape(rows, -1), flat_index, axis=1)
    speeds = jnp.take(speed_one.reshape(rows, -1), flat_index, axis=1).astype(jnp.float32)
    product = jnp.where(inside, values * speeds, 0.0).reshape(rows, wall_count, 2)
    return jnp.sum(product, axis=2)


def on_device(
    adjoint,
    checkpoints,
    checkpoint_step,
    metric,
    helmholtz_inverse,
    wall_element,
    wall_local,
    wall_weight,
):
    planes_dev = adjoint.shape[1]
    elems_dev = adjoint.shape[3]
    wall_count = wall_element.shape[0]
    span_count = lax.axis_size("span")
    share = elems_dev // span_count
    all_modes = lax.all_gather(helmholtz_inverse, "span", axis=0, tiled=True)
    offset = lax.axis_index("plane") * elems_dev
    local_element = wall_element - offset
    inside = ((local_element >= 0) & (local_element < elems_dev)).reshape(-1)
    flat_index = (wall_local * elems_dev + jnp.clip(local_element, 0, elems_dev - 1)).reshape(-1)
    velocity = jnp.stack([
        lax.dynamic_index_in_dim(checkpoints, checkpoint_step[s], 0, keepdims=False)
        for s in range(NSTEP)
    ])
    velocity = lax.all_to_all(velocity, "span", split_axis=4, concat_axis=2, tiled=True)
    field = lax.all_to_all(adjoint, "span", split_axis=3, concat_axis=1, tiled=True)
    scale = lax.dynamic_slice_in_dim(metric, lax.axis_index("span") * share, share, 1)
    product = 0.0
    for substep in range(NSTEP):
        advected = transport(field, velocity[substep], scale)
        field = backward_planes(solve_modes(all_modes, forward_modes(advected)))
        product = product + field[1] * velocity[substep, 1].astype(jnp.float32)
    both = to_plane_layout(jnp.concatenate([field, product[None]], axis=0))
    gathered = jnp.take(both[3].reshape(planes_dev, -1), flat_index, axis=1)
    partial_sum = jnp.where(inside, gathered, 0.0).reshape(planes_dev, wall_count, 2).sum(axis=2)
    weighted = wall_weight * partial_sum
    grad_share = lax.psum_scatter(weighted, "plane", scatter_dimension=1, tiled=True)
    square_total = lax.psum(jnp.sum(grad_share * grad_share), ("span", "plane"))
    inverse_rms = lax.rsqrt(square_total / (planes_dev * span_count * wall_count) + 1e-06)
    return (both[:3], grad_share * inverse_rms)


MESH = pl.DeviceIdType.MESH
F32 = jnp.float32
BF16 = jnp.bfloat16
LANES = 128


def swap_blocks(parts, share):
    count = len(parts)
    width = count * share
    lane = lax.broadcasted_iota(jnp.int32, parts[0].shape, 1)
    k = count // 2
    while k:
        upper = (lane // (k * share)) % 2 == 1
        new = list(parts)
        for i in range(count):
            if (i // k) % 2 == 0:
                a, b = parts[i], parts[i + k]
                new[i] = jnp.where(upper, pltpu.roll(b, k * share, 1), a)
                new[i + k] = jnp.where(upper, b, pltpu.roll(a, width - k * share, 1))
        parts = new
        k //= 2
    return parts


def greet(spans, planes):
    me, p = lax.axis_index("span"), lax.axis_index("plane")
    barrier = pltpu.get_barrier_semaphore()
    for o in range(1, spans):
        pl.semaphore_signal(barrier, 1, device_id={"span": (me + o) % spans}, device_id_type=MESH)
    for o in range(1, planes):
        pl.semaphore_signal(barrier, 1, device_id={"plane": (p + o) % planes}, device_id_type=MESH)
    pl.semaphore_wait(barrier, spans + planes - 2)


def remote(src, dst, sems, kind, o, target):
    return pltpu.make_async_remote_copy(
        src_ref=src, dst_ref=dst, send_sem=sems.at[0, kind, o], recv_sem=sems.at[1, kind, o],
        device_id=target, device_id_type=MESH,
    )


def step_kernel(spans, planes, zdev, q, qp,
                step_ref, adj_ref, ck_ref, inv_ref, metric_ref, elem_ref, local_ref, weight_ref,
                basis_ref, diff_ref, place_ref,
                back, weighted_ref, trcv,
                xs_ref, vs_ref, modes_ref, tail, snd, rcv, vsnd, vrcv,
                coef, solved, product, modes_hi, modes_lo, bsnd,
                wall, rows_in, part, wrcv, square, srcv, total, sems, local_sem):
    share = LANES // spans
    me, p = lax.axis_index("span"), lax.axis_index("plane")
    bulk = q - 1
    half = bulk // 2
    slabs = 3 * zdev
    sets = 2 * slabs // spans
    greet(spans, planes)

    def span_to(o):
        return {"span": (me + o) % spans}

    xpeer = {"plane": (p + 2) % planes}
    cpeer = {"plane": p + 1 - 2 * (p % 2)}
    px = (p + 2) % planes
    pc = p + 1 - 2 * (p % 2)
    pcx = (pc + 2) % planes
    stage1, stage2x, stage2c, stage3 = [], [], [], []
    for o in range(1, spans):
        s = (me + spans - o) % spans
        out = remote(inv_ref.at[p], modes_ref.at[p, me], sems, 0, o, span_to(o))
        out.start()
        stage1.append((out, remote(inv_ref.at[p], modes_ref.at[p, s], sems, 0, o, span_to(o))))
        stage2x.append((remote(modes_ref.at[p, s], modes_ref.at[p, s], sems, 1, o, xpeer),
                        remote(modes_ref.at[p, s], modes_ref.at[px, s], sems, 1, o, xpeer)))
        stage2c.append((remote(modes_ref.at[p, s], modes_ref.at[p, s], sems, 2, o, cpeer),
                        remote(modes_ref.at[p, s], modes_ref.at[pc, s], sems, 2, o, cpeer)))
        stage3.append((remote(modes_ref.at[px, s], modes_ref.at[px, s], sems, 3, o, cpeer),
                       remote(modes_ref.at[px, s], modes_ref.at[pcx, s], sems, 3, o, cpeer)))

    tail[...] = jnp.zeros_like(tail)
    for k in range(slabs):
        tail[k % spans, k // spans:k // spans + 1, :] = adj_ref[k // zdev, k % zdev, bulk:q, :]
    for t in range(NSTEP):
        slot = step_ref[t]
        for k in range(2 * zdev):
            row = ck_ref[slot, k // zdev, k % zdev].astype(F32)[bulk:q, :]
            tail[k, 2 + t:3 + t, :] = row
    for i in range(sets):
        parts = []
        for g in range(spans):
            h = spans * i + g
            k, r = h // 2, (h % 2) * half
            parts.append(adj_ref[k // zdev, k % zdev, r:r + half, :])
        parts = swap_blocks(parts, share)
        for d in range(spans):
            snd[d, i * half:(i + 1) * half, :] = parts[d]
    parts = swap_blocks([tail[g] for g in range(spans)], share)
    for d in range(spans):
        snd[d, sets * half:, :] = parts[d]
    fields, speeds = [], [[] for _ in range(NSTEP)]
    for o in range(1, spans):
        to, s = (me + o) % spans, (me + spans - o) % spans
        out = remote(snd.at[to], rcv.at[me], sems, 4, o, span_to(o))
        out.start()
        fields.append((out, remote(snd.at[to], rcv.at[s], sems, 4, o, span_to(o))))
    own = pltpu.make_async_copy(snd.at[me], rcv.at[me], local_sem.at[0])
    own.start()
    wide = zdev * LANES
    for t in range(NSTEP):
        slot = step_ref[t]
        parts = [ck_ref[slot, k // zdev, k % zdev].astype(F32)[:bulk] for k in range(2 * zdev)]
        parts = swap_blocks(parts, share)
        for d in range(spans):
            vsnd[d, t] = parts[d].astype(BF16)
        for o in range(1, spans):
            to, s = (me + o) % spans, (me + spans - o) % spans
            out = remote(vsnd.at[to, t], vrcv.at[me, t], sems, 5 + t, o, span_to(o))
            out.start()
            speeds[t].append((out, remote(vsnd.at[to, t], vrcv.at[s, t], sems, 5 + t, o, span_to(o))))
    vown = pltpu.make_async_copy(vsnd.at[me], vrcv.at[me], local_sem.at[1])
    vown.start()
    mine = [pltpu.make_async_copy(inv_ref.at[j], modes_ref.at[j, me], local_sem.at[2 + j])
            for j in range(zdev)]
    for c in mine:
        c.start()
    xs_ref[bulk:, :] = jnp.zeros_like(xs_ref[bulk:, :])
    vs_ref[:, :, bulk:, :] = jnp.zeros_like(vs_ref[:, :, bulk:, :])
    product[...] = jnp.zeros_like(product)
    lane = lax.broadcasted_iota(jnp.int32, (1, LANES), 1)
    rolled = pltpu.roll(metric_ref[...], (LANES - me * share) % LANES, 1)
    scale = jnp.where(lane < share, rolled, 0.0)
    k = share
    while k < LANES:
        scale = scale + pltpu.roll(scale, k, 1)
        k *= 2
    block = lax.broadcasted_iota(jnp.int32, (1, 3 * LANES), 1) % LANES // share
    first = jnp.concatenate([scale[0:1]] * zdev, axis=1)
    second = jnp.concatenate([scale[1:2]] * zdev, axis=1)

    for o in range(spans - 1):
        stage1[o][1].wait_recv()
        stage2x[o][0].start()
        stage2c[o][0].start()
    for o in range(spans - 1):
        stage2x[o][1].wait_recv()
        stage3[o][0].start()
    own.wait()
    for c in fields:
        c[1].wait_recv()
    for i in range(sets):
        parts = swap_blocks([rcv[s, i * half:(i + 1) * half, :] for s in range(spans)], share)
        for g in range(spans):
            h = spans * i + g
            k, r = h // 2, (h % 2) * half
            xs_ref[r:r + half, k * LANES:(k + 1) * LANES] = parts[g]
    parts = swap_blocks([rcv[s, sets * half:, :] for s in range(spans)], share)
    for k in range(slabs):
        xs_ref[bulk:q, k * LANES:(k + 1) * LANES] = parts[k % spans][k // spans:k // spans + 1]
    for t in range(NSTEP):
        for k in range(2 * zdev):
            z = k % zdev
            vs_ref[t, k // zdev, bulk:q, z * LANES:(z + 1) * LANES] = parts[k][2 + t:3 + t]
    vown.wait()

    for t in range(NSTEP):
        for c in speeds[t]:
            c[1].wait_recv()
        parts = swap_blocks([vrcv[s, t].astype(F32) for s in range(spans)], share)
        for k in range(2 * zdev):
            z = k % zdev
            vs_ref[t, k // zdev, :bulk, z * LANES:(z + 1) * LANES] = parts[k]
        v0 = vs_ref[t, 0] * first
        v1 = vs_ref[t, 1] * second
        for c in range(3):
            x = xs_ref[:, c * wide:(c + 1) * wide]
            d = mul3((diff_ref[0], diff_ref[1]), split(x))
            coef[c * qp:(c + 1) * qp, :] = x + v0 * d[:qp] + v1 * d[qp:]
        y = mul3(split(coef[...]), (basis_ref[0], basis_ref[1]))
        coef[...] = y
        if t == 0:
            for c in mine:
                c.wait()
            for group in (stage2c, stage3):
                for c in group:
                    c[1].wait_recv()
            for j in range(zdev):
                for s in range(spans):
                    high, low = split(modes_ref[j, s])
                    modes_hi[j, s * qp:(s + 1) * qp, :] = high
                    modes_lo[j, s * qp:(s + 1) * qp, :] = low
        for j in range(zdev):
            lanes = slice(j * LANES, (j + 1) * LANES)
            x = jnp.concatenate([coef[c * qp:(c + 1) * qp, lanes] for c in range(3)], axis=1)
            r = mul3((modes_hi[j, :, :qp], modes_lo[j, :, :qp]), split(x))
            acc = r[:qp]
            for s in range(1, spans):
                acc = jnp.where(block == s, r[s * qp:(s + 1) * qp], acc)
            for c in range(3):
                solved[c * qp:(c + 1) * qp, lanes] = acc[:, c * LANES:(c + 1) * LANES]
        y = mul3(split(solved[...]), (basis_ref[0], basis_ref[1]), ((1,), (1,)))
        for c in range(3):
            xs_ref[:, c * wide:(c + 1) * wide] = y[c * qp:(c + 1) * qp]
        product[...] += y[qp:2 * qp] * vs_ref[t, 1]

    def exchange(kind, size, axis, pick_src, dst):
        at = lax.axis_index(axis)
        pairs = []
        for o in range(1, size):
            to, s = (at + o) % size, (at + size - o) % size
            out = remote(pick_src(to), dst.at[at], sems, kind, o, {axis: to})
            out.start()
            pairs.append((out, remote(pick_src(to), dst.at[s], sems, kind, o, {axis: to})))
        return pairs

    high, low = split(product[...].T)
    base = p * LANES + me * share
    mode = lax.broadcasted_iota(jnp.int32, (qp, LANES), 0)
    near = lax.broadcasted_iota(jnp.int32, (LANES, LANES), 0) % share + base
    for piece in range(planes):
        acc = 0.0
        for h in range(2):
            lo = (piece * 2 + h) * LANES
            got = 0.0
            for k in range(2):
                pick = jnp.where(local_ref[k:k + 1, lo:lo + LANES] == mode, 1.0, 0.0).astype(BF16)
                keep = jnp.where(elem_ref[k:k + 1, lo:lo + LANES] == near, 1.0, 0.0)
                keep = jnp.concatenate([keep] * zdev, axis=0)
                one = jnp.dot(high, pick, preferred_element_type=F32)
                one = one + jnp.dot(low, pick, preferred_element_type=F32)
                got = got + one * keep
            for v in split(got):
                acc = acc + jnp.dot(place_ref[h], v, preferred_element_type=F32)
        for s in range(spans):
            wall[piece, s] = acc[s * 8:(s + 1) * 8]
    rows = exchange(8, planes, "plane", lambda to: wall.at[to], rows_in)
    rown = pltpu.make_async_copy(wall.at[p], rows_in.at[p], local_sem.at[0])
    rown.start()

    for k in range(slabs):
        tail[k % spans, k // spans:k // spans + 1, :] = xs_ref[bulk:q, k * LANES:(k + 1) * LANES]
    for i in range(sets):
        parts = []
        for g in range(spans):
            h = spans * i + g
            k, r = h // 2, (h % 2) * half
            parts.append(xs_ref[r:r + half, k * LANES:(k + 1) * LANES])
        parts = swap_blocks(parts, share)
        for d in range(spans):
            bsnd[d, i * half:(i + 1) * half, :] = parts[d]
    parts = swap_blocks([tail[g] for g in range(spans)], share)
    for d in range(spans):
        bsnd[d, sets * half:, :] = parts[d]
    rown.wait()
    for c in rows:
        c[1].wait_recv()
    part[...] = sum(rows_in[s] for s in range(planes))
    walls = exchange(9, spans, "span", lambda to: part.at[to], wrcv)
    returned = exchange(10, spans, "span", lambda to: bsnd.at[to], back)
    bown = pltpu.make_async_copy(bsnd.at[me], back.at[me], local_sem.at[1])
    bown.start()
    wown = pltpu.make_async_copy(part.at[me], wrcv.at[me], local_sem.at[0])
    wown.start()
    wown.wait()
    for c in walls:
        c[1].wait_recv()
    both = sum(wrcv[s] for s in range(spans))
    sums = jnp.concatenate([both[:zdev], both[zdev:]], axis=1)
    weight = weight_ref[:, pl.ds(pl.multiple_of(p * 2 * LANES, 2 * LANES), 2 * LANES)]
    weighted = weight * sums
    weighted_ref[...] = weighted
    sq = weighted * weighted
    square[...] = jnp.broadcast_to(jnp.sum(sq[:, :LANES] + sq[:, LANES:], axis=0, keepdims=True), (8, LANES))
    squares = exchange(11, spans, "span", lambda to: square, srcv)
    srcv[me] = square[...]
    for c in squares:
        c[1].wait_recv()
    total[...] = sum(srcv[s] for s in range(spans))
    totals = exchange(12, planes, "plane", lambda to: total, trcv)
    trcv[p] = total[...]
    for c in totals:
        c[1].wait_recv()
    bown.wait()
    for c in returned:
        c[1].wait_recv()
    for group in (stage1, stage2x, stage2c, stage3, fields, *speeds, rows, walls, returned, squares, totals):
        for c in group:
            c[0].wait_send()


def split(x):
    high = x.astype(BF16)
    return high, (x - high.astype(F32)).astype(BF16)


def mul3(a, b, dims=((1,), (0,))):
    def one(x, y):
        return lax.dot_general(x, y, (dims, ((), ())), preferred_element_type=F32)
    return one(a[0], b[0]) + (one(a[0], b[1]) + one(a[1], b[0]))


def finish_kernel(spans, planes, zdev, q, count, back, weighted_ref, trcv, out_ref, grad_ref):
    share = LANES // spans
    bulk = q - 1
    half = bulk // 2
    slabs = 3 * zdev
    sets = 2 * slabs // spans
    full = jnp.sum(sum(trcv[s] for s in range(planes))[0:1], axis=1, keepdims=True)
    grad_ref[...] = weighted_ref[...] * lax.rsqrt(full / count + 1e-06)
    for i in range(sets):
        parts = swap_blocks([back[s, i * half:(i + 1) * half, :] for s in range(spans)], share)
        for g in range(spans):
            h = spans * i + g
            k, r = h // 2, (h % 2) * half
            out_ref[k // zdev, r:r + half, k % zdev, :] = parts[g]
    parts = swap_blocks([back[s, sets * half:, :] for s in range(spans)], share)
    for k in range(slabs):
        out_ref[k // zdev, bulk:q, k % zdev, :] = parts[k % spans][k // spans:k // spans + 1]


def halves(table):
    high = table.astype(np.float32).astype(ml_dtypes.bfloat16)
    low = (table - high.astype(np.float64)).astype(np.float32).astype(ml_dtypes.bfloat16)
    return np.stack([high, low])


def tables(spans, zdev, q, qp):
    share = LANES // spans
    fourier = fourier_table(spans * zdev)
    order = np.array([s * zdev + z for z in range(zdev) for s in range(spans)])
    basis = np.kron(fourier[order][:, order].T, np.eye(share))
    side = P_SIZE + 1
    matrix = chebyshev_matrix(P_SIZE)
    diff = np.zeros((2 * qp, qp))
    diff[:q, :q] = np.kron(matrix, np.eye(side))
    diff[qp:qp + q, :q] = np.kron(np.eye(side), matrix)
    place = np.zeros((2, spans * 8, zdev * LANES), ml_dtypes.bfloat16)
    for h in range(2):
        for s in range(spans):
            for z in range(zdev):
                at = z * LANES + s * share
                place[h, s * 8 + h * zdev + z, at:at + share] = 1.0
    return halves(basis), halves(diff), place


def vmem(n):
    return [pl.BlockSpec(memory_space=pltpu.VMEM)] * n


def kernels_on_device(spans, planes, adjoint, checkpoints, checkpoint_step, metric,
                      helmholtz_inverse, wall_element, wall_local, wall_weight):
    _, zdev, q, _ = adjoint.shape
    wall_count = wall_element.shape[0]
    qp = -(-q // 16) * 16
    bulk, wide = q - 1, zdev * LANES
    rows = 3 * zdev * bulk // spans + 8
    inverse = jnp.pad(helmholtz_inverse, ((0, 0), (0, qp - q), (0, LANES - q)))
    shape = jax.ShapeDtypeStruct
    basis, diff, place = tables(spans, zdev, q, qp)
    back, weighted, squares = pl.pallas_call(
        functools.partial(step_kernel, spans, planes, zdev, q, qp),
        out_shape=(shape((spans, rows, LANES), F32), shape((zdev, wall_count // planes), F32),
                   shape((planes, 8, LANES), F32)),
        in_specs=[pl.BlockSpec(memory_space=pltpu.SMEM)] + vmem(10),
        out_specs=tuple(vmem(3)),
        scratch_shapes=[
            pltpu.VMEM((qp, 3 * wide), F32),
            pltpu.VMEM((NSTEP, 2, qp, wide), F32),
            pltpu.VMEM((zdev, spans, qp, LANES), F32),
            pltpu.VMEM((spans, 8, LANES), F32),
            pltpu.VMEM((spans, rows, LANES), F32),
            pltpu.VMEM((spans, rows, LANES), F32),
            pltpu.VMEM((spans, NSTEP, bulk, LANES), BF16),
            pltpu.VMEM((spans, NSTEP, bulk, LANES), BF16),
            pltpu.VMEM((3 * qp, wide), F32),
            pltpu.VMEM((3 * qp, wide), F32),
            pltpu.VMEM((qp, wide), F32),
            pltpu.VMEM((zdev, spans * qp, LANES), BF16),
            pltpu.VMEM((zdev, spans * qp, LANES), BF16),
            pltpu.VMEM((spans, rows, LANES), F32),
            pltpu.VMEM((planes, spans, 8, LANES), F32),
            pltpu.VMEM((planes, spans, 8, LANES), F32),
            pltpu.VMEM((spans, 8, LANES), F32),
            pltpu.VMEM((spans, 8, LANES), F32),
            pltpu.VMEM((8, LANES), F32),
            pltpu.VMEM((spans, 8, LANES), F32),
            pltpu.VMEM((8, LANES), F32),
            pltpu.SemaphoreType.DMA((2, 13, spans)),
            pltpu.SemaphoreType.DMA((2 + zdev,)),
        ],
        compiler_params=pltpu.CompilerParams(collective_id=0, has_side_effects=True),
        name="steps",
    )(checkpoint_step, adjoint, checkpoints, inverse, metric, wall_element.T, wall_local.T,
      wall_weight, basis, diff, place)
    field, gradient = pl.pallas_call(
        functools.partial(finish_kernel, spans, planes, zdev, q, float(spans * zdev * wall_count)),
        out_shape=(shape((3, q, zdev, LANES), F32), shape((zdev, wall_count // planes), F32)),
        in_specs=vmem(3),
        out_specs=tuple(vmem(2)),
        name="finish",
    )(back, weighted, squares)
    return field.transpose(0, 2, 1, 3), gradient


def chosen(spans, planes, *args):
    zdev, q, elems = args[0].shape[1:]
    walls = args[5].shape[0]
    fits = (
        elems == LANES and spans == 2 * zdev and planes == zdev == 4
        and walls == planes * 2 * LANES and q % 16 == 1 and q < LANES
    )
    if fits:
        return kernels_on_device(spans, planes, *args)
    return on_device(*args)


def solution(mesh):
    placed = (
        P(None, "span", None, "plane"),
        P(None, None, "span", None, "plane"),
        P(),
        P(None, "plane"),
        P("span", None, None),
        P(),
        P(),
        P("span", None),
    )
    return jax.shard_map(
        functools.partial(chosen, mesh.shape["span"], mesh.shape["plane"]),
        mesh=mesh,
        in_specs=placed,
        out_specs=(P(None, "span", None, "plane"), P("span", "plane")),
        check_vma=False,
    )
```

```python
import functools

import jax
import jax.numpy as jnp
import ml_dtypes
import numpy as np
from jax import lax
from jax.experimental import pallas as pl
from jax.experimental.pallas import tpu as pltpu
from jax.sharding import PartitionSpec as P

P_SIZE = 8
NSTEP = 3


HIGHEST = lax.Precision.HIGHEST


def chebyshev_matrix(degree):
    points = np.arange(degree + 1)
    abscissa = np.cos(np.pi * points / degree)
    signed = np.where((points == 0) | (points == degree), 2.0, 1.0) * (-1.0) ** points
    spacing = abscissa[:, None] - abscissa[None, :] + np.eye(degree + 1)
    matrix = signed[:, None] / signed[None, :] / spacing
    return matrix - np.eye(degree + 1) * np.sum(matrix, axis=1)[:, None]


def fourier_table(length):
    row_index = np.arange(length)[:, None]
    column = np.arange(length)[None, :]
    wavenumber = (row_index + 1) // 2
    phase_angle = 2.0 * np.pi * wavenumber * column / length
    parity = row_index % 2
    base_rows = np.where(
        row_index == 0, 1.0, np.where(parity == 1, np.cos(phase_angle), np.sin(phase_angle))
    )
    row_scale = np.where(
        (row_index == 0) | (row_index == length - 1), 1.0 / np.sqrt(length), np.sqrt(2.0 / length)
    )
    return base_rows * row_scale


def transport(field_data, velocity, metric):
    side_nodes = P_SIZE + 1
    matrix = jnp.asarray(chebyshev_matrix(P_SIZE), jnp.float32)
    shaped = field_data.reshape(
        field_data.shape[0], field_data.shape[1], side_nodes, side_nodes, field_data.shape[3]
    )
    first_dir = jnp.einsum("ai,czibe->czabe", matrix, shaped, precision=HIGHEST).reshape(
        field_data.shape
    )
    second_dir = jnp.einsum("bi,czaie->czabe", matrix, shaped, precision=HIGHEST).reshape(
        field_data.shape
    )
    speed_data = velocity.astype(jnp.float32)
    return (
        field_data
        + speed_data[0] * (metric[0] * first_dir)
        + speed_data[1] * (metric[1] * second_dir)
    )


def forward_modes(gathered):
    basis_table = jnp.asarray(fourier_table(gathered.shape[1]), jnp.float32)
    return jnp.einsum("jz,czqe->cjqe", basis_table, gathered, precision=HIGHEST)


def backward_planes(solved):
    basis_table = jnp.asarray(fourier_table(solved.shape[1]), jnp.float32)
    return jnp.einsum("jz,cjqe->czqe", basis_table, solved, precision=HIGHEST)


def solve_modes(inverse_block, coefficients):
    return jnp.einsum("jqr,cjre->cjqe", inverse_block, coefficients, precision=HIGHEST)


def to_plane_layout(point_data):
    return lax.all_to_all(point_data, "span", split_axis=1, concat_axis=3, tiled=True)


def wall_terms(field_one, speed_one, flat_index, inside, wall_count):
    rows = field_one.shape[0]
    values = jnp.take(field_one.reshape(rows, -1), flat_index, axis=1)
    speeds = jnp.take(speed_one.reshape(rows, -1), flat_index, axis=1).astype(jnp.float32)
    product = jnp.where(inside, values * speeds, 0.0).reshape(rows, wall_count, 2)
    return jnp.sum(product, axis=2)


def on_device(
    adjoint,
    checkpoints,
    checkpoint_step,
    metric,
    helmholtz_inverse,
    wall_element,
    wall_local,
    wall_weight,
):
    planes_dev = adjoint.shape[1]
    elems_dev = adjoint.shape[3]
    wall_count = wall_element.shape[0]
    span_count = lax.axis_size("span")
    share = elems_dev // span_count
    all_modes = lax.all_gather(helmholtz_inverse, "span", axis=0, tiled=True)
    offset = lax.axis_index("plane") * elems_dev
    local_element = wall_element - offset
    inside = ((local_element >= 0) & (local_element < elems_dev)).reshape(-1)
    flat_index = (wall_local * elems_dev + jnp.clip(local_element, 0, elems_dev - 1)).reshape(-1)
    velocity = jnp.stack([
        lax.dynamic_index_in_dim(checkpoints, checkpoint_step[s], 0, keepdims=False)
        for s in range(NSTEP)
    ])
    velocity = lax.all_to_all(velocity, "span", split_axis=4, concat_axis=2, tiled=True)
    field = lax.all_to_all(adjoint, "span", split_axis=3, concat_axis=1, tiled=True)
    scale = lax.dynamic_slice_in_dim(metric, lax.axis_index("span") * share, share, 1)
    product = 0.0
    for substep in range(NSTEP):
        advected = transport(field, velocity[substep], scale)
        field = backward_planes(solve_modes(all_modes, forward_modes(advected)))
        product = product + field[1] * velocity[substep, 1].astype(jnp.float32)
    both = to_plane_layout(jnp.concatenate([field, product[None]], axis=0))
    gathered = jnp.take(both[3].reshape(planes_dev, -1), flat_index, axis=1)
    partial_sum = jnp.where(inside, gathered, 0.0).reshape(planes_dev, wall_count, 2).sum(axis=2)
    weighted = wall_weight * partial_sum
    grad_share = lax.psum_scatter(weighted, "plane", scatter_dimension=1, tiled=True)
    square_total = lax.psum(jnp.sum(grad_share * grad_share), ("span", "plane"))
    inverse_rms = lax.rsqrt(square_total / (planes_dev * span_count * wall_count) + 1e-06)
    return (both[:3], grad_share * inverse_rms)


MESH = pl.DeviceIdType.MESH
F32 = jnp.float32
BF16 = jnp.bfloat16
LANES = 128


def swap_blocks(parts, share):
    count = len(parts)
    width = count * share
    lane = lax.broadcasted_iota(jnp.int32, parts[0].shape, 1)
    k = count // 2
    while k:
        upper = (lane // (k * share)) % 2 == 1
        new = list(parts)
        for i in range(count):
            if (i // k) % 2 == 0:
                a, b = parts[i], parts[i + k]
                new[i] = jnp.where(upper, pltpu.roll(b, k * share, 1), a)
                new[i + k] = jnp.where(upper, b, pltpu.roll(a, width - k * share, 1))
        parts = new
        k //= 2
    return parts


def coded(x):
    top = jnp.maximum(jnp.max(jnp.abs(x), axis=0, keepdims=True), 1e-30)
    return jnp.round(x * (32767.0 / top)).astype(jnp.int32), top * (1.0 / 32767.0)


def coded_blocks(rows, sets, half):
    pairs = [coded(rows[i * half:(i + 1) * half]) for i in range(sets)]
    whole = jnp.concatenate([a for a, _ in pairs], axis=0)
    return whole.astype(jnp.int16), [b for _, b in pairs]


def decoded(x, scale):
    return x.astype(jnp.int32).astype(F32) * scale


def greet(spans, planes):
    me, p = lax.axis_index("span"), lax.axis_index("plane")
    barrier = pltpu.get_barrier_semaphore()
    for o in range(1, spans):
        pl.semaphore_signal(barrier, 1, device_id={"span": (me + o) % spans}, device_id_type=MESH)
    for o in range(1, planes):
        pl.semaphore_signal(barrier, 1, device_id={"plane": (p + o) % planes}, device_id_type=MESH)
    pl.semaphore_wait(barrier, spans + planes - 2)


def remote(src, dst, sems, kind, o, target):
    return pltpu.make_async_remote_copy(
        src_ref=src, dst_ref=dst, send_sem=sems.at[0, kind, o], recv_sem=sems.at[1, kind, o],
        device_id=target, device_id_type=MESH,
    )


def step_kernel(spans, planes, zdev, q, qp,
                step_ref, adj_ref, ck_ref, inv_ref, metric_ref, elem_ref, local_ref, weight_ref,
                basis_ref, diff_ref, place_ref,
                back, tback, weighted_ref, trcv,
                xs_ref, vs_ref, padded, inv16, modes_ref, tail, stage, snd, tsnd, rcv, trc, vsnd, vrcv,
                coef, solved, product, modes_hi, modes_lo, bsnd, tbsnd,
                wall, rows_in, part, wrcv, square, srcv, total, sems, local_sem):
    share = LANES // spans
    me, p = lax.axis_index("span"), lax.axis_index("plane")
    bulk = q - 1
    half = bulk // 2
    slabs = 3 * zdev
    sets = 2 * slabs // spans
    greet(spans, planes)

    def span_to(o):
        return {"span": (me + o) % spans}

    eye = (lax.broadcasted_iota(jnp.int32, (qp, LANES), 0)
           == lax.broadcasted_iota(jnp.int32, (qp, LANES), 1))
    padded[...] = jnp.zeros_like(padded)
    extra = []
    for j in range(zdev):
        padded[:q, :q] = inv_ref[:, j, :]
        x = padded[...]
        whole, scale = coded(jnp.where(eye, 0.0, x))
        inv16[j] = whole.astype(jnp.int16)
        extra.append((scale, jnp.sum(jnp.where(eye, x, 0.0), axis=0, keepdims=True)))
    xpeer = {"plane": (p + 2) % planes}
    cpeer = {"plane": p + 1 - 2 * (p % 2)}
    px = (p + 2) % planes
    pc = p + 1 - 2 * (p % 2)
    pcx = (pc + 2) % planes
    stage1, stage2x, stage2c, stage3 = [], [], [], []
    for o in range(1, spans):
        s = (me + spans - o) % spans
        out = remote(inv16.at[p], modes_ref.at[p, me], sems, 0, o, span_to(o))
        out.start()
        stage1.append((out, remote(inv16.at[p], modes_ref.at[p, s], sems, 0, o, span_to(o))))
        stage2x.append((remote(modes_ref.at[p, s], modes_ref.at[p, s], sems, 1, o, xpeer),
                        remote(modes_ref.at[p, s], modes_ref.at[px, s], sems, 1, o, xpeer)))
        stage2c.append((remote(modes_ref.at[p, s], modes_ref.at[p, s], sems, 2, o, cpeer),
                        remote(modes_ref.at[p, s], modes_ref.at[pc, s], sems, 2, o, cpeer)))
        stage3.append((remote(modes_ref.at[px, s], modes_ref.at[px, s], sems, 3, o, cpeer),
                       remote(modes_ref.at[px, s], modes_ref.at[pcx, s], sems, 3, o, cpeer)))

    tail[...] = jnp.zeros_like(tail)
    for k in range(slabs):
        tail[k % spans, k // spans:k // spans + 1, :] = adj_ref[k // zdev, k % zdev, bulk:q, :]
    for t in range(NSTEP):
        slot = step_ref[t]
        for k in range(2 * zdev):
            row = ck_ref[slot, k // zdev, k % zdev].astype(F32)[bulk:q, :]
            tail[k, 2 + t:3 + t, :] = row
    for i in range(sets):
        parts = []
        for g in range(spans):
            h = spans * i + g
            k, r = h // 2, (h % 2) * half
            parts.append(adj_ref[k // zdev, k % zdev, r:r + half, :])
        parts = swap_blocks(parts, share)
        for d in range(spans):
            stage[d, i * half:(i + 1) * half, :] = parts[d]
    parts = swap_blocks([tail[g] for g in range(spans)], share)
    more = jnp.concatenate([a for a, _ in extra] + [b for _, b in extra], axis=0)
    for d in range(spans):
        snd[d], scales = coded_blocks(stage[d], sets, half)
        tsnd[d, :8] = jnp.concatenate([parts[d][:5]] + scales, axis=0)
        tsnd[d, 8:] = more
    tails = []
    fields, speeds = [], [[] for _ in range(NSTEP)]
    for o in range(1, spans):
        to, s = (me + o) % spans, (me + spans - o) % spans
        out = remote(snd.at[to], rcv.at[me], sems, 4, o, span_to(o))
        out.start()
        fields.append((out, remote(snd.at[to], rcv.at[s], sems, 4, o, span_to(o))))
        out = remote(tsnd.at[to], trc.at[me], sems, 13, o, span_to(o))
        out.start()
        tails.append((out, remote(tsnd.at[to], trc.at[s], sems, 13, o, span_to(o))))
    own = pltpu.make_async_copy(snd.at[me], rcv.at[me], local_sem.at[0])
    own.start()
    town = pltpu.make_async_copy(tsnd.at[me], trc.at[me], local_sem.at[2 + zdev])
    town.start()
    wide = zdev * LANES
    for t in range(NSTEP):
        slot = step_ref[t]
        parts = [ck_ref[slot, k // zdev, k % zdev].astype(F32)[:bulk] for k in range(2 * zdev)]
        parts = swap_blocks(parts, share)
        for d in range(spans):
            vsnd[d, t] = parts[d].astype(BF16)
        for o in range(1, spans):
            to, s = (me + o) % spans, (me + spans - o) % spans
            out = remote(vsnd.at[to, t], vrcv.at[me, t], sems, 5 + t, o, span_to(o))
            out.start()
            speeds[t].append((out, remote(vsnd.at[to, t], vrcv.at[s, t], sems, 5 + t, o, span_to(o))))
    vown = pltpu.make_async_copy(vsnd.at[me], vrcv.at[me], local_sem.at[1])
    vown.start()
    mine = [pltpu.make_async_copy(inv16.at[j], modes_ref.at[j, me], local_sem.at[2 + j])
            for j in range(zdev)]
    for c in mine:
        c.start()
    xs_ref[bulk:, :] = jnp.zeros_like(xs_ref[bulk:, :])
    vs_ref[:, :, bulk:, :] = jnp.zeros_like(vs_ref[:, :, bulk:, :])
    product[...] = jnp.zeros_like(product)
    lane = lax.broadcasted_iota(jnp.int32, (1, LANES), 1)
    rolled = pltpu.roll(metric_ref[...], (LANES - me * share) % LANES, 1)
    scale = jnp.where(lane < share, rolled, 0.0)
    k = share
    while k < LANES:
        scale = scale + pltpu.roll(scale, k, 1)
        k *= 2
    block = lax.broadcasted_iota(jnp.int32, (1, 3 * LANES), 1) % LANES // share
    first = jnp.concatenate([scale[0:1]] * zdev, axis=1)
    second = jnp.concatenate([scale[1:2]] * zdev, axis=1)

    for o in range(spans - 1):
        stage1[o][1].wait_recv()
        stage2x[o][0].start()
        stage2c[o][0].start()
    for o in range(spans - 1):
        stage2x[o][1].wait_recv()
        stage3[o][0].start()
    own.wait()
    town.wait()
    for c in fields + tails:
        c[1].wait_recv()
    for s in range(spans):
        x = rcv[s].astype(jnp.int32).astype(F32)
        for i in range(sets):
            stage[s, i * half:(i + 1) * half, :] = x[i * half:(i + 1) * half] * trc[s, 5 + i:6 + i, :]
    for i in range(sets):
        parts = swap_blocks([stage[s, i * half:(i + 1) * half, :] for s in range(spans)], share)
        for g in range(spans):
            h = spans * i + g
            k, r = h // 2, (h % 2) * half
            xs_ref[r:r + half, k * LANES:(k + 1) * LANES] = parts[g]
    parts = swap_blocks([trc[s, :8, :] for s in range(spans)], share)
    for k in range(slabs):
        xs_ref[bulk:q, k * LANES:(k + 1) * LANES] = parts[k % spans][k // spans:k // spans + 1]
    for t in range(NSTEP):
        for k in range(2 * zdev):
            z = k % zdev
            vs_ref[t, k // zdev, bulk:q, z * LANES:(z + 1) * LANES] = parts[k][2 + t:3 + t]
    vown.wait()

    for t in range(NSTEP):
        for c in speeds[t]:
            c[1].wait_recv()
        parts = swap_blocks([vrcv[s, t].astype(F32) for s in range(spans)], share)
        for k in range(2 * zdev):
            z = k % zdev
            vs_ref[t, k // zdev, :bulk, z * LANES:(z + 1) * LANES] = parts[k]
        v0 = vs_ref[t, 0] * first
        v1 = vs_ref[t, 1] * second
        for c in range(3):
            x = xs_ref[:, c * wide:(c + 1) * wide]
            d = mul3((diff_ref[0], diff_ref[1]), split(x))
            coef[c * qp:(c + 1) * qp, :] = x + v0 * d[:qp] + v1 * d[qp:]
        y = mul3(split(coef[...]), (basis_ref[0], basis_ref[1]))
        coef[...] = y
        if t == 0:
            for c in mine:
                c.wait()
            for group in (stage2c, stage3):
                for c in group:
                    c[1].wait_recv()
            for j in range(zdev):
                for s in range(spans):
                    x = decoded(modes_ref[j, s], trc[s, 8 + j:9 + j, :])
                    x = jnp.where(eye, trc[s, 8 + zdev + j:9 + zdev + j, :], x)
                    high, low = split(x)
                    modes_hi[j, s * qp:(s + 1) * qp, :] = high
                    modes_lo[j, s * qp:(s + 1) * qp, :] = low
        for j in range(zdev):
            lanes = slice(j * LANES, (j + 1) * LANES)
            x = jnp.concatenate([coef[c * qp:(c + 1) * qp, lanes] for c in range(3)], axis=1)
            r = mul3((modes_hi[j, :, :qp], modes_lo[j, :, :qp]), split(x))
            acc = r[:qp]
            for s in range(1, spans):
                acc = jnp.where(block == s, r[s * qp:(s + 1) * qp], acc)
            for c in range(3):
                solved[c * qp:(c + 1) * qp, lanes] = acc[:, c * LANES:(c + 1) * LANES]
        y = mul3(split(solved[...]), (basis_ref[0], basis_ref[1]), ((1,), (1,)))
        for c in range(3):
            xs_ref[:, c * wide:(c + 1) * wide] = y[c * qp:(c + 1) * qp]
        product[...] += y[qp:2 * qp] * vs_ref[t, 1]

    def exchange(kind, size, axis, pick_src, dst):
        at = lax.axis_index(axis)
        pairs = []
        for o in range(1, size):
            to, s = (at + o) % size, (at + size - o) % size
            out = remote(pick_src(to), dst.at[at], sems, kind, o, {axis: to})
            out.start()
            pairs.append((out, remote(pick_src(to), dst.at[s], sems, kind, o, {axis: to})))
        return pairs

    high, low = split(product[...].T)
    base = p * LANES + me * share
    mode = lax.broadcasted_iota(jnp.int32, (qp, LANES), 0)
    near = lax.broadcasted_iota(jnp.int32, (LANES, LANES), 0) % share + base
    for piece in range(planes):
        acc = 0.0
        for h in range(2):
            lo = (piece * 2 + h) * LANES
            got = 0.0
            for k in range(2):
                pick = jnp.where(local_ref[k:k + 1, lo:lo + LANES] == mode, 1.0, 0.0).astype(BF16)
                keep = jnp.where(elem_ref[k:k + 1, lo:lo + LANES] == near, 1.0, 0.0)
                keep = jnp.concatenate([keep] * zdev, axis=0)
                one = jnp.dot(high, pick, preferred_element_type=F32)
                one = one + jnp.dot(low, pick, preferred_element_type=F32)
                got = got + one * keep
            for v in split(got):
                acc = acc + jnp.dot(place_ref[h], v, preferred_element_type=F32)
        for s in range(spans):
            wall[piece, s] = acc[s * 8:(s + 1) * 8]
    rows = exchange(8, planes, "plane", lambda to: wall.at[to], rows_in)
    rown = pltpu.make_async_copy(wall.at[p], rows_in.at[p], local_sem.at[0])
    rown.start()

    for k in range(slabs):
        tail[k % spans, k // spans:k // spans + 1, :] = xs_ref[bulk:q, k * LANES:(k + 1) * LANES]
    for i in range(sets):
        parts = []
        for g in range(spans):
            h = spans * i + g
            k, r = h // 2, (h % 2) * half
            parts.append(xs_ref[r:r + half, k * LANES:(k + 1) * LANES])
        parts = swap_blocks(parts, share)
        for d in range(spans):
            stage[d, i * half:(i + 1) * half, :] = parts[d]
    parts = swap_blocks([tail[g] for g in range(spans)], share)
    for d in range(spans):
        bsnd[d], scales = coded_blocks(stage[d], sets, half)
        tbsnd[d] = jnp.concatenate([parts[d][:5]] + scales, axis=0)
    rown.wait()
    for c in rows:
        c[1].wait_recv()
    part[...] = sum(rows_in[s] for s in range(planes))
    walls = exchange(9, spans, "span", lambda to: part.at[to], wrcv)
    returned = exchange(10, spans, "span", lambda to: bsnd.at[to], back)
    returned += exchange(14, spans, "span", lambda to: tbsnd.at[to], tback)
    tbown = pltpu.make_async_copy(tbsnd.at[me], tback.at[me], local_sem.at[2])
    tbown.start()
    bown = pltpu.make_async_copy(bsnd.at[me], back.at[me], local_sem.at[1])
    bown.start()
    wown = pltpu.make_async_copy(part.at[me], wrcv.at[me], local_sem.at[0])
    wown.start()
    wown.wait()
    for c in walls:
        c[1].wait_recv()
    both = sum(wrcv[s] for s in range(spans))
    sums = jnp.concatenate([both[:zdev], both[zdev:]], axis=1)
    weight = weight_ref[:, pl.ds(pl.multiple_of(p * 2 * LANES, 2 * LANES), 2 * LANES)]
    weighted = weight * sums
    weighted_ref[...] = weighted
    sq = weighted * weighted
    square[...] = jnp.broadcast_to(jnp.sum(sq[:, :LANES] + sq[:, LANES:], axis=0, keepdims=True), (8, LANES))
    squares = exchange(11, spans, "span", lambda to: square, srcv)
    srcv[me] = square[...]
    for c in squares:
        c[1].wait_recv()
    total[...] = sum(srcv[s] for s in range(spans))
    totals = exchange(12, planes, "plane", lambda to: total, trcv)
    trcv[p] = total[...]
    for c in totals:
        c[1].wait_recv()
    bown.wait()
    tbown.wait()
    for c in returned:
        c[1].wait_recv()
    for group in (stage1, stage2x, stage2c, stage3, fields, tails, *speeds, rows, walls, returned, squares, totals):
        for c in group:
            c[0].wait_send()


def split(x):
    high = x.astype(BF16)
    return high, (x - high.astype(F32)).astype(BF16)


def mul3(a, b, dims=((1,), (0,))):
    def one(x, y):
        return lax.dot_general(x, y, (dims, ((), ())), preferred_element_type=F32)
    return one(a[0], b[0]) + (one(a[0], b[1]) + one(a[1], b[0]))


def finish_kernel(spans, planes, zdev, q, count, back, tback, weighted_ref, trcv, out_ref, grad_ref, stage):
    share = LANES // spans
    bulk = q - 1
    half = bulk // 2
    slabs = 3 * zdev
    sets = 2 * slabs // spans
    full = jnp.sum(sum(trcv[s] for s in range(planes))[0:1], axis=1, keepdims=True)
    grad_ref[...] = weighted_ref[...] * lax.rsqrt(full / count + 1e-06)
    for s in range(spans):
        x = back[s].astype(jnp.int32).astype(F32)
        for i in range(sets):
            stage[s, i * half:(i + 1) * half, :] = x[i * half:(i + 1) * half] * tback[s, 5 + i:6 + i, :]
    for i in range(sets):
        parts = swap_blocks([stage[s, i * half:(i + 1) * half, :] for s in range(spans)], share)
        for g in range(spans):
            h = spans * i + g
            k, r = h // 2, (h % 2) * half
            out_ref[k // zdev, r:r + half, k % zdev, :] = parts[g]
    parts = swap_blocks([tback[s] for s in range(spans)], share)
    for k in range(slabs):
        out_ref[k // zdev, bulk:q, k % zdev, :] = parts[k % spans][k // spans:k // spans + 1]


def halves(table):
    high = table.astype(np.float32).astype(ml_dtypes.bfloat16)
    low = (table - high.astype(np.float64)).astype(np.float32).astype(ml_dtypes.bfloat16)
    return np.stack([high, low])


def tables(spans, zdev, q, qp):
    share = LANES // spans
    fourier = fourier_table(spans * zdev)
    order = np.array([s * zdev + z for z in range(zdev) for s in range(spans)])
    basis = np.kron(fourier[order][:, order].T, np.eye(share))
    side = P_SIZE + 1
    matrix = chebyshev_matrix(P_SIZE)
    diff = np.zeros((2 * qp, qp))
    diff[:q, :q] = np.kron(matrix, np.eye(side))
    diff[qp:qp + q, :q] = np.kron(np.eye(side), matrix)
    place = np.zeros((2, spans * 8, zdev * LANES), ml_dtypes.bfloat16)
    for h in range(2):
        for s in range(spans):
            for z in range(zdev):
                at = z * LANES + s * share
                place[h, s * 8 + h * zdev + z, at:at + share] = 1.0
    return halves(basis), halves(diff), place


def vmem(n):
    return [pl.BlockSpec(memory_space=pltpu.VMEM)] * n


def kernels_on_device(spans, planes, adjoint, checkpoints, checkpoint_step, metric,
                      helmholtz_inverse, wall_element, wall_local, wall_weight):
    _, zdev, q, _ = adjoint.shape
    wall_count = wall_element.shape[0]
    qp = -(-q // 16) * 16
    bulk, wide = q - 1, zdev * LANES
    rows = 3 * zdev * bulk // spans
    inverse = helmholtz_inverse.transpose(1, 0, 2)
    shape = jax.ShapeDtypeStruct
    basis, diff, place = tables(spans, zdev, q, qp)
    back, tback, weighted, squares = pl.pallas_call(
        functools.partial(step_kernel, spans, planes, zdev, q, qp),
        out_shape=(shape((spans, rows, LANES), jnp.int16), shape((spans, 8, LANES), F32),
                   shape((zdev, wall_count // planes), F32),
                   shape((planes, 8, LANES), F32)),
        in_specs=[pl.BlockSpec(memory_space=pltpu.SMEM)] + vmem(10),
        out_specs=tuple(vmem(4)),
        scratch_shapes=[
            pltpu.VMEM((qp, 3 * wide), F32),
            pltpu.VMEM((NSTEP, 2, qp, wide), F32),
            pltpu.VMEM((qp, LANES), F32),
            pltpu.VMEM((zdev, qp, LANES), jnp.int16),
            pltpu.VMEM((zdev, spans, qp, LANES), jnp.int16),
            pltpu.VMEM((spans, 8, LANES), F32),
            pltpu.VMEM((spans, rows, LANES), F32),
            pltpu.VMEM((spans, rows, LANES), jnp.int16),
            pltpu.VMEM((spans, 8 + 2 * zdev, LANES), F32),
            pltpu.VMEM((spans, rows, LANES), jnp.int16),
            pltpu.VMEM((spans, 8 + 2 * zdev, LANES), F32),
            pltpu.VMEM((spans, NSTEP, bulk, LANES), BF16),
            pltpu.VMEM((spans, NSTEP, bulk, LANES), BF16),
            pltpu.VMEM((3 * qp, wide), F32),
            pltpu.VMEM((3 * qp, wide), F32),
            pltpu.VMEM((qp, wide), F32),
            pltpu.VMEM((zdev, spans * qp, LANES), BF16),
            pltpu.VMEM((zdev, spans * qp, LANES), BF16),
            pltpu.VMEM((spans, rows, LANES), jnp.int16),
            pltpu.VMEM((spans, 8, LANES), F32),
            pltpu.VMEM((planes, spans, 8, LANES), F32),
            pltpu.VMEM((planes, spans, 8, LANES), F32),
            pltpu.VMEM((spans, 8, LANES), F32),
            pltpu.VMEM((spans, 8, LANES), F32),
            pltpu.VMEM((8, LANES), F32),
            pltpu.VMEM((spans, 8, LANES), F32),
            pltpu.VMEM((8, LANES), F32),
            pltpu.SemaphoreType.DMA((2, 15, spans)),
            pltpu.SemaphoreType.DMA((3 + zdev,)),
        ],
        compiler_params=pltpu.CompilerParams(collective_id=0, has_side_effects=True),
        name="steps",
    )(checkpoint_step, adjoint, checkpoints, inverse, metric, wall_element.T, wall_local.T,
      wall_weight, basis, diff, place)
    field, gradient = pl.pallas_call(
        functools.partial(finish_kernel, spans, planes, zdev, q, float(spans * zdev * wall_count)),
        out_shape=(shape((3, q, zdev, LANES), F32), shape((zdev, wall_count // planes), F32)),
        in_specs=vmem(4),
        out_specs=tuple(vmem(2)),
        scratch_shapes=[pltpu.VMEM((spans, rows, LANES), F32)],
        name="finish",
    )(back, tback, weighted, squares)
    return field.transpose(0, 2, 1, 3), gradient


def chosen(spans, planes, *args):
    zdev, q, elems = args[0].shape[1:]
    walls = args[5].shape[0]
    fits = (
        elems == LANES and spans == 2 * zdev and planes == zdev == 4
        and walls == planes * 2 * LANES and q % 16 == 1 and q < LANES
    )
    if fits:
        return kernels_on_device(spans, planes, *args)
    return on_device(*args)


def solution(mesh):
    placed = (
        P(None, "span", None, "plane"),
        P(None, None, "span", None, "plane"),
        P(),
        P(None, "plane"),
        P("span", None, None),
        P(),
        P(),
        P("span", None),
    )
    return jax.shard_map(
        functools.partial(chosen, mesh.shape["span"], mesh.shape["plane"]),
        mesh=mesh,
        in_specs=placed,
        out_specs=(P(None, "span", None, "plane"), P("span", "plane")),
        check_vma=False,
    )
```

```python
import functools

import jax
import jax.numpy as jnp
import ml_dtypes
import numpy as np
from jax import lax
from jax.experimental import pallas as pl
from jax.experimental.pallas import tpu as pltpu
from jax.sharding import PartitionSpec as P

P_SIZE = 8
NSTEP = 3


HIGHEST = lax.Precision.HIGHEST


def chebyshev_matrix(degree):
    points = np.arange(degree + 1)
    abscissa = np.cos(np.pi * points / degree)
    signed = np.where((points == 0) | (points == degree), 2.0, 1.0) * (-1.0) ** points
    spacing = abscissa[:, None] - abscissa[None, :] + np.eye(degree + 1)
    matrix = signed[:, None] / signed[None, :] / spacing
    return matrix - np.eye(degree + 1) * np.sum(matrix, axis=1)[:, None]


def fourier_table(length):
    row_index = np.arange(length)[:, None]
    column = np.arange(length)[None, :]
    wavenumber = (row_index + 1) // 2
    phase_angle = 2.0 * np.pi * wavenumber * column / length
    parity = row_index % 2
    base_rows = np.where(
        row_index == 0, 1.0, np.where(parity == 1, np.cos(phase_angle), np.sin(phase_angle))
    )
    row_scale = np.where(
        (row_index == 0) | (row_index == length - 1), 1.0 / np.sqrt(length), np.sqrt(2.0 / length)
    )
    return base_rows * row_scale


def transport(field_data, velocity, metric):
    side_nodes = P_SIZE + 1
    matrix = jnp.asarray(chebyshev_matrix(P_SIZE), jnp.float32)
    shaped = field_data.reshape(
        field_data.shape[0], field_data.shape[1], side_nodes, side_nodes, field_data.shape[3]
    )
    first_dir = jnp.einsum("ai,czibe->czabe", matrix, shaped, precision=HIGHEST).reshape(
        field_data.shape
    )
    second_dir = jnp.einsum("bi,czaie->czabe", matrix, shaped, precision=HIGHEST).reshape(
        field_data.shape
    )
    speed_data = velocity.astype(jnp.float32)
    return (
        field_data
        + speed_data[0] * (metric[0] * first_dir)
        + speed_data[1] * (metric[1] * second_dir)
    )


def forward_modes(gathered):
    basis_table = jnp.asarray(fourier_table(gathered.shape[1]), jnp.float32)
    return jnp.einsum("jz,czqe->cjqe", basis_table, gathered, precision=HIGHEST)


def backward_planes(solved):
    basis_table = jnp.asarray(fourier_table(solved.shape[1]), jnp.float32)
    return jnp.einsum("jz,cjqe->czqe", basis_table, solved, precision=HIGHEST)


def solve_modes(inverse_block, coefficients):
    return jnp.einsum("jqr,cjre->cjqe", inverse_block, coefficients, precision=HIGHEST)


def to_plane_layout(point_data):
    return lax.all_to_all(point_data, "span", split_axis=1, concat_axis=3, tiled=True)


def wall_terms(field_one, speed_one, flat_index, inside, wall_count):
    rows = field_one.shape[0]
    values = jnp.take(field_one.reshape(rows, -1), flat_index, axis=1)
    speeds = jnp.take(speed_one.reshape(rows, -1), flat_index, axis=1).astype(jnp.float32)
    product = jnp.where(inside, values * speeds, 0.0).reshape(rows, wall_count, 2)
    return jnp.sum(product, axis=2)


def on_device(
    adjoint,
    checkpoints,
    checkpoint_step,
    metric,
    helmholtz_inverse,
    wall_element,
    wall_local,
    wall_weight,
):
    planes_dev = adjoint.shape[1]
    elems_dev = adjoint.shape[3]
    wall_count = wall_element.shape[0]
    span_count = lax.axis_size("span")
    share = elems_dev // span_count
    all_modes = lax.all_gather(helmholtz_inverse, "span", axis=0, tiled=True)
    offset = lax.axis_index("plane") * elems_dev
    local_element = wall_element - offset
    inside = ((local_element >= 0) & (local_element < elems_dev)).reshape(-1)
    flat_index = (wall_local * elems_dev + jnp.clip(local_element, 0, elems_dev - 1)).reshape(-1)
    velocity = jnp.stack([
        lax.dynamic_index_in_dim(checkpoints, checkpoint_step[s], 0, keepdims=False)
        for s in range(NSTEP)
    ])
    velocity = lax.all_to_all(velocity, "span", split_axis=4, concat_axis=2, tiled=True)
    field = lax.all_to_all(adjoint, "span", split_axis=3, concat_axis=1, tiled=True)
    scale = lax.dynamic_slice_in_dim(metric, lax.axis_index("span") * share, share, 1)
    product = 0.0
    for substep in range(NSTEP):
        advected = transport(field, velocity[substep], scale)
        field = backward_planes(solve_modes(all_modes, forward_modes(advected)))
        product = product + field[1] * velocity[substep, 1].astype(jnp.float32)
    both = to_plane_layout(jnp.concatenate([field, product[None]], axis=0))
    gathered = jnp.take(both[3].reshape(planes_dev, -1), flat_index, axis=1)
    partial_sum = jnp.where(inside, gathered, 0.0).reshape(planes_dev, wall_count, 2).sum(axis=2)
    weighted = wall_weight * partial_sum
    grad_share = lax.psum_scatter(weighted, "plane", scatter_dimension=1, tiled=True)
    square_total = lax.psum(jnp.sum(grad_share * grad_share), ("span", "plane"))
    inverse_rms = lax.rsqrt(square_total / (planes_dev * span_count * wall_count) + 1e-06)
    return (both[:3], grad_share * inverse_rms)


MESH = pl.DeviceIdType.MESH
F32 = jnp.float32
BF16 = jnp.bfloat16
LANES = 128


def swap_blocks(parts, share):
    count = len(parts)
    width = count * share
    lane = lax.broadcasted_iota(jnp.int32, parts[0].shape, 1)
    k = count // 2
    while k:
        upper = (lane // (k * share)) % 2 == 1
        new = list(parts)
        for i in range(count):
            if (i // k) % 2 == 0:
                a, b = parts[i], parts[i + k]
                new[i] = jnp.where(upper, pltpu.roll(b, k * share, 1), a)
                new[i + k] = jnp.where(upper, b, pltpu.roll(a, width - k * share, 1))
        parts = new
        k //= 2
    return parts


def coded(x):
    top = jnp.maximum(jnp.max(jnp.abs(x), axis=0, keepdims=True), 1e-30)
    return jnp.round(x * (32767.0 / top)).astype(jnp.int32), top * (1.0 / 32767.0)


def coded_blocks(rows, sets, half):
    pairs = [coded(rows[i * half:(i + 1) * half]) for i in range(sets)]
    whole = jnp.concatenate([a for a, _ in pairs], axis=0)
    return whole.astype(jnp.int16), [b for _, b in pairs]


def decoded(x, scale):
    return x.astype(jnp.int32).astype(F32) * scale


def greet(spans, planes):
    me, p = lax.axis_index("span"), lax.axis_index("plane")
    barrier = pltpu.get_barrier_semaphore()
    for o in range(1, spans):
        pl.semaphore_signal(barrier, 1, device_id={"span": (me + o) % spans}, device_id_type=MESH)
    for o in range(1, planes):
        pl.semaphore_signal(barrier, 1, device_id={"plane": (p + o) % planes}, device_id_type=MESH)
    pl.semaphore_wait(barrier, spans + planes - 2)


def remote(src, dst, sems, kind, o, target):
    return pltpu.make_async_remote_copy(
        src_ref=src, dst_ref=dst, send_sem=sems.at[0, kind, o], recv_sem=sems.at[1, kind, o],
        device_id=target, device_id_type=MESH,
    )


def step_kernel(spans, planes, zdev, q, qp,
                step_ref, adj_ref, ck_ref, inv_ref, metric_ref, elem_ref, local_ref, weight_ref,
                basis_ref, diff_ref, place_ref,
                back, tback, weighted_ref, trcv,
                xs_ref, vs_ref, padded, inv16, modes_ref, tail, stage, snd, tsnd, rcv, trc, vsnd, vrcv,
                coef, solved, product, modes_cat, bsnd, tbsnd,
                wall, rows_in, part, wrcv, square, srcv, total, sems, local_sem):
    share = LANES // spans
    me, p = lax.axis_index("span"), lax.axis_index("plane")
    bulk = q - 1
    half = bulk // 2
    slabs = 3 * zdev
    sets = 2 * slabs // spans
    greet(spans, planes)

    def span_to(o):
        return {"span": (me + o) % spans}

    eye = (lax.broadcasted_iota(jnp.int32, (qp, LANES), 0)
           == lax.broadcasted_iota(jnp.int32, (qp, LANES), 1))
    padded[...] = jnp.zeros_like(padded)
    extra = []
    for j in range(zdev):
        padded[:q, :q] = inv_ref[:, j, :]
        x = padded[...]
        whole, scale = coded(jnp.where(eye, 0.0, x))
        inv16[j] = whole.astype(jnp.int16)
        extra.append((scale, jnp.sum(jnp.where(eye, x, 0.0), axis=0, keepdims=True)))
    xpeer = {"plane": (p + 2) % planes}
    cpeer = {"plane": p + 1 - 2 * (p % 2)}
    px = (p + 2) % planes
    pc = p + 1 - 2 * (p % 2)
    pcx = (pc + 2) % planes
    stage1, stage2x, stage2c, stage3 = [], [], [], []
    for o in range(1, spans):
        s = (me + spans - o) % spans
        out = remote(inv16.at[p], modes_ref.at[p, me], sems, 0, o, span_to(o))
        out.start()
        stage1.append((out, remote(inv16.at[p], modes_ref.at[p, s], sems, 0, o, span_to(o))))
        stage2x.append((remote(modes_ref.at[p, s], modes_ref.at[p, s], sems, 1, o, xpeer),
                        remote(modes_ref.at[p, s], modes_ref.at[px, s], sems, 1, o, xpeer)))
        stage2c.append((remote(modes_ref.at[p, s], modes_ref.at[p, s], sems, 2, o, cpeer),
                        remote(modes_ref.at[p, s], modes_ref.at[pc, s], sems, 2, o, cpeer)))
        stage3.append((remote(modes_ref.at[px, s], modes_ref.at[px, s], sems, 3, o, cpeer),
                       remote(modes_ref.at[px, s], modes_ref.at[pcx, s], sems, 3, o, cpeer)))

    tail[...] = jnp.zeros_like(tail)
    for k in range(slabs):
        tail[k % spans, k // spans:k // spans + 1, :] = adj_ref[k // zdev, k % zdev, bulk:q, :]
    for t in range(NSTEP):
        slot = step_ref[t]
        for k in range(2 * zdev):
            row = ck_ref[slot, k // zdev, k % zdev].astype(F32)[bulk:q, :]
            tail[k, 2 + t:3 + t, :] = row
    for i in range(sets):
        parts = []
        for g in range(spans):
            h = spans * i + g
            k, r = h // 2, (h % 2) * half
            parts.append(adj_ref[k // zdev, k % zdev, r:r + half, :])
        parts = swap_blocks(parts, share)
        for d in range(spans):
            stage[d, i * half:(i + 1) * half, :] = parts[d]
    parts = swap_blocks([tail[g] for g in range(spans)], share)
    more = jnp.concatenate([a for a, _ in extra] + [b for _, b in extra], axis=0)
    for d in range(spans):
        snd[d], scales = coded_blocks(stage[d], sets, half)
        tsnd[d, :8] = jnp.concatenate([parts[d][:5]] + scales, axis=0)
        tsnd[d, 8:] = more
    tails = []
    fields, speeds = [], [[] for _ in range(NSTEP)]
    for o in range(1, spans):
        to, s = (me + o) % spans, (me + spans - o) % spans
        out = remote(snd.at[to], rcv.at[me], sems, 4, o, span_to(o))
        out.start()
        fields.append((out, remote(snd.at[to], rcv.at[s], sems, 4, o, span_to(o))))
        out = remote(tsnd.at[to], trc.at[me], sems, 13, o, span_to(o))
        out.start()
        tails.append((out, remote(tsnd.at[to], trc.at[s], sems, 13, o, span_to(o))))
    own = pltpu.make_async_copy(snd.at[me], rcv.at[me], local_sem.at[0])
    own.start()
    town = pltpu.make_async_copy(tsnd.at[me], trc.at[me], local_sem.at[2 + zdev])
    town.start()
    wide = zdev * LANES
    for t in range(NSTEP):
        slot = step_ref[t]
        parts = [ck_ref[slot, k // zdev, k % zdev].astype(F32)[:bulk] for k in range(2 * zdev)]
        parts = swap_blocks(parts, share)
        for d in range(spans):
            vsnd[d, t] = parts[d].astype(BF16)
        for o in range(1, spans):
            to, s = (me + o) % spans, (me + spans - o) % spans
            out = remote(vsnd.at[to, t], vrcv.at[me, t], sems, 5 + t, o, span_to(o))
            out.start()
            speeds[t].append((out, remote(vsnd.at[to, t], vrcv.at[s, t], sems, 5 + t, o, span_to(o))))
    vown = pltpu.make_async_copy(vsnd.at[me], vrcv.at[me], local_sem.at[1])
    vown.start()
    mine = [pltpu.make_async_copy(inv16.at[j], modes_ref.at[j, me], local_sem.at[2 + j])
            for j in range(zdev)]
    for c in mine:
        c.start()
    xs_ref[bulk:, :] = jnp.zeros_like(xs_ref[bulk:, :])
    vs_ref[:, :, bulk:, :] = jnp.zeros_like(vs_ref[:, :, bulk:, :])
    product[...] = jnp.zeros_like(product)
    lane = lax.broadcasted_iota(jnp.int32, (1, LANES), 1)
    rolled = pltpu.roll(metric_ref[...], (LANES - me * share) % LANES, 1)
    scale = jnp.where(lane < share, rolled, 0.0)
    k = share
    while k < LANES:
        scale = scale + pltpu.roll(scale, k, 1)
        k *= 2
    block = lax.broadcasted_iota(jnp.int32, (1, 3 * LANES), 1) % LANES // share
    gap = jnp.zeros((LANES - qp, 3 * LANES), BF16)
    first = jnp.concatenate([scale[0:1]] * zdev, axis=1)
    second = jnp.concatenate([scale[1:2]] * zdev, axis=1)

    for o in range(spans - 1):
        stage1[o][1].wait_recv()
        stage2x[o][0].start()
        stage2c[o][0].start()
    for o in range(spans - 1):
        stage2x[o][1].wait_recv()
        stage3[o][0].start()
    own.wait()
    town.wait()
    for c in fields + tails:
        c[1].wait_recv()
    for s in range(spans):
        x = rcv[s].astype(jnp.int32).astype(F32)
        for i in range(sets):
            stage[s, i * half:(i + 1) * half, :] = x[i * half:(i + 1) * half] * trc[s, 5 + i:6 + i, :]
    for i in range(sets):
        parts = swap_blocks([stage[s, i * half:(i + 1) * half, :] for s in range(spans)], share)
        for g in range(spans):
            h = spans * i + g
            k, r = h // 2, (h % 2) * half
            xs_ref[r:r + half, k * LANES:(k + 1) * LANES] = parts[g]
    parts = swap_blocks([trc[s, :8, :] for s in range(spans)], share)
    for k in range(slabs):
        xs_ref[bulk:q, k * LANES:(k + 1) * LANES] = parts[k % spans][k // spans:k // spans + 1]
    for t in range(NSTEP):
        for k in range(2 * zdev):
            z = k % zdev
            vs_ref[t, k // zdev, bulk:q, z * LANES:(z + 1) * LANES] = parts[k][2 + t:3 + t]
    vown.wait()

    for t in range(NSTEP):
        for c in speeds[t]:
            c[1].wait_recv()
        parts = swap_blocks([vrcv[s, t].astype(F32) for s in range(spans)], share)
        for k in range(2 * zdev):
            z = k % zdev
            vs_ref[t, k // zdev, :bulk, z * LANES:(z + 1) * LANES] = parts[k]
        v0 = vs_ref[t, 0] * first
        v1 = vs_ref[t, 1] * second
        for c in range(3):
            x = xs_ref[:, c * wide:(c + 1) * wide]
            high, low = split(x)
            d = dot(diff_ref[...], jnp.concatenate([high, low, high], axis=0))
            coef[c * qp:(c + 1) * qp, :] = x + v0 * d[:qp] + v1 * d[qp:]
        y = transform(coef[...], basis_ref, False)
        coef[...] = y
        if t == 0:
            for c in mine:
                c.wait()
            for group in (stage2c, stage3):
                for c in group:
                    c[1].wait_recv()
            for j in range(zdev):
                for s in range(spans):
                    x = decoded(modes_ref[j, s], trc[s, 8 + j:9 + j, :])
                    x = jnp.where(eye, trc[s, 8 + zdev + j:9 + zdev + j, :], x)
                    high, low = split(x)
                    modes_cat[j, s * qp:(s + 1) * qp, :LANES] = high
                    modes_cat[j, s * qp:(s + 1) * qp, LANES:2 * LANES] = high
                    modes_cat[j, s * qp:(s + 1) * qp, 2 * LANES:] = low
        for j in range(zdev):
            lanes = slice(j * LANES, (j + 1) * LANES)
            x = jnp.concatenate([coef[c * qp:(c + 1) * qp, lanes] for c in range(3)], axis=1)
            high, low = split(x)
            r = dot(modes_cat[j], jnp.concatenate([high, gap, low, gap, high, gap], axis=0))
            acc = r[:qp]
            for s in range(1, spans):
                acc = jnp.where(block == s, r[s * qp:(s + 1) * qp], acc)
            for c in range(3):
                solved[c * qp:(c + 1) * qp, lanes] = acc[:, c * LANES:(c + 1) * LANES]
        y = transform(solved[...], basis_ref, True)
        for c in range(3):
            xs_ref[:, c * wide:(c + 1) * wide] = y[c * qp:(c + 1) * qp]
        product[...] += y[qp:2 * qp] * vs_ref[t, 1]

    def exchange(kind, size, axis, pick_src, dst):
        at = lax.axis_index(axis)
        pairs = []
        for o in range(1, size):
            to, s = (at + o) % size, (at + size - o) % size
            out = remote(pick_src(to), dst.at[at], sems, kind, o, {axis: to})
            out.start()
            pairs.append((out, remote(pick_src(to), dst.at[s], sems, kind, o, {axis: to})))
        return pairs

    for k in range(slabs):
        tail[k % spans, k // spans:k // spans + 1, :] = xs_ref[bulk:q, k * LANES:(k + 1) * LANES]
    for i in range(sets):
        parts = []
        for g in range(spans):
            h = spans * i + g
            k, r = h // 2, (h % 2) * half
            parts.append(xs_ref[r:r + half, k * LANES:(k + 1) * LANES])
        parts = swap_blocks(parts, share)
        for d in range(spans):
            stage[d, i * half:(i + 1) * half, :] = parts[d]
    parts = swap_blocks([tail[g] for g in range(spans)], share)
    for d in range(spans):
        bsnd[d], scales = coded_blocks(stage[d], sets, half)
        tbsnd[d] = jnp.concatenate([parts[d][:5]] + scales, axis=0)
    returned = exchange(10, spans, "span", lambda to: bsnd.at[to], back)
    returned += exchange(14, spans, "span", lambda to: tbsnd.at[to], tback)
    tbown = pltpu.make_async_copy(tbsnd.at[me], tback.at[me], local_sem.at[2])
    tbown.start()
    bown = pltpu.make_async_copy(bsnd.at[me], back.at[me], local_sem.at[1])
    bown.start()
    high, low = split(product[...].T)
    left = jnp.concatenate([high, low], axis=1)
    pair = 2 * LANES
    base = p * LANES + me * share
    mode = lax.broadcasted_iota(jnp.int32, (qp, pair), 0)
    near = lax.broadcasted_iota(jnp.int32, (LANES, pair), 0) % share + base
    for piece in range(planes):
        lanes = slice(piece * pair, (piece + 1) * pair)
        got = 0.0
        for k in range(2):
            pick = jnp.where(local_ref[k:k + 1, lanes] == mode, 1.0, 0.0).astype(BF16)
            keep = jnp.where(elem_ref[k:k + 1, lanes] == near, 1.0, 0.0)
            keep = jnp.concatenate([keep] * zdev, axis=0)
            got = got + dot(left, jnp.concatenate([pick, pick], axis=0)) * keep
        acc = dot(place_ref[...], jnp.concatenate(split(got), axis=0))
        acc = acc[:, :LANES] + pltpu.roll(acc[:, LANES:], zdev, 0)
        for s in range(spans):
            wall[piece, s] = acc[s * 8:(s + 1) * 8]
    rows = exchange(8, planes, "plane", lambda to: wall.at[to], rows_in)
    rown = pltpu.make_async_copy(wall.at[p], rows_in.at[p], local_sem.at[0])
    rown.start()

    rown.wait()
    for c in rows:
        c[1].wait_recv()
    part[...] = sum(rows_in[s] for s in range(planes))
    walls = exchange(9, spans, "span", lambda to: part.at[to], wrcv)
    wown = pltpu.make_async_copy(part.at[me], wrcv.at[me], local_sem.at[0])
    wown.start()
    wown.wait()
    for c in walls:
        c[1].wait_recv()
    both = sum(wrcv[s] for s in range(spans))
    sums = jnp.concatenate([both[:zdev], both[zdev:]], axis=1)
    weight = weight_ref[:, pl.ds(pl.multiple_of(p * 2 * LANES, 2 * LANES), 2 * LANES)]
    weighted = weight * sums
    weighted_ref[...] = weighted
    sq = weighted * weighted
    square[...] = jnp.broadcast_to(jnp.sum(sq[:, :LANES] + sq[:, LANES:], axis=0, keepdims=True), (8, LANES))
    squares = exchange(11, spans, "span", lambda to: square, srcv)
    srcv[me] = square[...]
    for c in squares:
        c[1].wait_recv()
    total[...] = sum(srcv[s] for s in range(spans))
    totals = exchange(12, planes, "plane", lambda to: total, trcv)
    trcv[p] = total[...]
    for c in totals:
        c[1].wait_recv()
    bown.wait()
    tbown.wait()
    for c in returned:
        c[1].wait_recv()
    for group in (stage1, stage2x, stage2c, stage3, fields, tails, *speeds, rows, walls, returned, squares, totals):
        for c in group:
            c[0].wait_send()


def split(x):
    high = x.astype(BF16)
    return high, (x - high.astype(F32)).astype(BF16)


def dot(a, b, dims=((1,), (0,))):
    return lax.dot_general(a, b, (dims, ((), ())), preferred_element_type=F32)


def transform(x, basis_ref, back):
    high, low = split(x)
    left = jnp.concatenate([high, high, low], axis=1)
    parts = [basis_ref[0], basis_ref[1], basis_ref[0]]
    right = jnp.concatenate(parts, axis=1 if back else 0)
    return dot(left, right, ((1,), (1,)) if back else ((1,), (0,)))


def finish_kernel(spans, planes, zdev, q, count, back, tback, weighted_ref, trcv, out_ref, grad_ref, stage):
    share = LANES // spans
    bulk = q - 1
    half = bulk // 2
    slabs = 3 * zdev
    sets = 2 * slabs // spans
    full = jnp.sum(sum(trcv[s] for s in range(planes))[0:1], axis=1, keepdims=True)
    grad_ref[...] = weighted_ref[...] * lax.rsqrt(full / count + 1e-06)
    for s in range(spans):
        x = back[s].astype(jnp.int32).astype(F32)
        for i in range(sets):
            stage[s, i * half:(i + 1) * half, :] = x[i * half:(i + 1) * half] * tback[s, 5 + i:6 + i, :]
    for i in range(sets):
        parts = swap_blocks([stage[s, i * half:(i + 1) * half, :] for s in range(spans)], share)
        for g in range(spans):
            h = spans * i + g
            k, r = h // 2, (h % 2) * half
            out_ref[k // zdev, r:r + half, k % zdev, :] = parts[g]
    parts = swap_blocks([tback[s] for s in range(spans)], share)
    for k in range(slabs):
        out_ref[k // zdev, bulk:q, k % zdev, :] = parts[k % spans][k // spans:k // spans + 1]


def halves(table):
    high = table.astype(np.float32).astype(ml_dtypes.bfloat16)
    low = (table - high.astype(np.float64)).astype(np.float32).astype(ml_dtypes.bfloat16)
    return np.stack([high, low])


def tables(spans, zdev, q, qp):
    share = LANES // spans
    fourier = fourier_table(spans * zdev)
    order = np.array([s * zdev + z for z in range(zdev) for s in range(spans)])
    basis = np.kron(fourier[order][:, order].T, np.eye(share))
    side = P_SIZE + 1
    matrix = chebyshev_matrix(P_SIZE)
    diff = np.zeros((2 * qp, qp))
    diff[:q, :q] = np.kron(matrix, np.eye(side))
    diff[qp:qp + q, :q] = np.kron(np.eye(side), matrix)
    place = np.zeros((spans * 8, zdev * LANES), ml_dtypes.bfloat16)
    for s in range(spans):
        for z in range(zdev):
            at = z * LANES + s * share
            place[s * 8 + z, at:at + share] = 1.0
    high, low = halves(diff)
    diff = np.concatenate([high, high, low], axis=1)
    place = np.concatenate([place, place], axis=1)
    return halves(basis), diff, place


def vmem(n):
    return [pl.BlockSpec(memory_space=pltpu.VMEM)] * n


def kernels_on_device(spans, planes, adjoint, checkpoints, checkpoint_step, metric,
                      helmholtz_inverse, wall_element, wall_local, wall_weight):
    _, zdev, q, _ = adjoint.shape
    wall_count = wall_element.shape[0]
    qp = -(-q // 16) * 16
    bulk, wide = q - 1, zdev * LANES
    rows = 3 * zdev * bulk // spans
    inverse = helmholtz_inverse.transpose(1, 0, 2)
    shape = jax.ShapeDtypeStruct
    basis, diff, place = tables(spans, zdev, q, qp)
    back, tback, weighted, squares = pl.pallas_call(
        functools.partial(step_kernel, spans, planes, zdev, q, qp),
        out_shape=(shape((spans, rows, LANES), jnp.int16), shape((spans, 8, LANES), F32),
                   shape((zdev, wall_count // planes), F32),
                   shape((planes, 8, LANES), F32)),
        in_specs=[pl.BlockSpec(memory_space=pltpu.SMEM)] + vmem(10),
        out_specs=tuple(vmem(4)),
        scratch_shapes=[
            pltpu.VMEM((qp, 3 * wide), F32),
            pltpu.VMEM((NSTEP, 2, qp, wide), F32),
            pltpu.VMEM((qp, LANES), F32),
            pltpu.VMEM((zdev, qp, LANES), jnp.int16),
            pltpu.VMEM((zdev, spans, qp, LANES), jnp.int16),
            pltpu.VMEM((spans, 8, LANES), F32),
            pltpu.VMEM((spans, rows, LANES), F32),
            pltpu.VMEM((spans, rows, LANES), jnp.int16),
            pltpu.VMEM((spans, 8 + 2 * zdev, LANES), F32),
            pltpu.VMEM((spans, rows, LANES), jnp.int16),
            pltpu.VMEM((spans, 8 + 2 * zdev, LANES), F32),
            pltpu.VMEM((spans, NSTEP, bulk, LANES), BF16),
            pltpu.VMEM((spans, NSTEP, bulk, LANES), BF16),
            pltpu.VMEM((3 * qp, wide), F32),
            pltpu.VMEM((3 * qp, wide), F32),
            pltpu.VMEM((qp, wide), F32),
            pltpu.VMEM((zdev, spans * qp, 3 * LANES), BF16),
            pltpu.VMEM((spans, rows, LANES), jnp.int16),
            pltpu.VMEM((spans, 8, LANES), F32),
            pltpu.VMEM((planes, spans, 8, LANES), F32),
            pltpu.VMEM((planes, spans, 8, LANES), F32),
            pltpu.VMEM((spans, 8, LANES), F32),
            pltpu.VMEM((spans, 8, LANES), F32),
            pltpu.VMEM((8, LANES), F32),
            pltpu.VMEM((spans, 8, LANES), F32),
            pltpu.VMEM((8, LANES), F32),
            pltpu.SemaphoreType.DMA((2, 15, spans)),
            pltpu.SemaphoreType.DMA((3 + zdev,)),
        ],
        compiler_params=pltpu.CompilerParams(collective_id=0, has_side_effects=True),
        name="steps",
    )(checkpoint_step, adjoint, checkpoints, inverse, metric, wall_element.T, wall_local.T,
      wall_weight, basis, diff, place)
    field, gradient = pl.pallas_call(
        functools.partial(finish_kernel, spans, planes, zdev, q, float(spans * zdev * wall_count)),
        out_shape=(shape((3, q, zdev, LANES), F32), shape((zdev, wall_count // planes), F32)),
        in_specs=vmem(4),
        out_specs=tuple(vmem(2)),
        scratch_shapes=[pltpu.VMEM((spans, rows, LANES), F32)],
        name="finish",
    )(back, tback, weighted, squares)
    return field.transpose(0, 2, 1, 3), gradient


def chosen(spans, planes, *args):
    zdev, q, elems = args[0].shape[1:]
    walls = args[5].shape[0]
    fits = (
        elems == LANES and spans == 2 * zdev and planes == zdev == 4
        and walls == planes * 2 * LANES and q % 16 == 1 and q < LANES
    )
    if fits:
        return kernels_on_device(spans, planes, *args)
    return on_device(*args)


def solution(mesh):
    placed = (
        P(None, "span", None, "plane"),
        P(None, None, "span", None, "plane"),
        P(),
        P(None, "plane"),
        P("span", None, None),
        P(),
        P(),
        P("span", None),
    )
    return jax.shard_map(
        functools.partial(chosen, mesh.shape["span"], mesh.shape["plane"]),
        mesh=mesh,
        in_specs=placed,
        out_specs=(P(None, "span", None, "plane"), P("span", "plane")),
        check_vma=False,
    )
```
